32 devices in a mesh: cls: 16 (over z, y, x), dp: 2 (over core).
Axes of the slice: x: 2, y: 2, z: 4, core: 2. Of those that a mesh axis runs over, the one named last changes fastest.
Arguments:
- images: bfloat16 [512, 4096], P(('cls', 'dp')), may hold values from -6 to 6
- references: bfloat16 [16, 72, 4096], P('cls'), may hold values from -1 to 1
- candidates: int32 [512, 8], P(('cls', 'dp')), may hold values from 0 to 15, all different within a row; in each aligned block of 16 rows (0 to 15, 16 to 31, ...) at most 12 rows name the same one
- inv_noise: bfloat16 [512], P(('cls', 'dp')), may hold values from 0.5 to 150
Outputs:
- class_sums: float32 [16, 72, 4096], P('cls', 'dp')
- class_weights: float32 [16, 72], P('cls', 'dp')
The draws below stay inside these ranges and needn't reach their ends.
Inputs may be any that keep to these rules, and one draw needn't show every extreme that they name: `candidates`: the classes of one row differ. In each aligned block of 16 rows (the rows of one device) no class is named by more than 12 rows, a bound that some block reaches.
All inputs are finite; a program needn't handle non-finite values.
Results may differ from the reference program's by a relative error of at most 0.006.
Values may be sent and summed in bfloat16 or wider, within the bound.
A program may use at most 64 MiB of HBM per device.

```python
import math
import jax
import jax.numpy as jnp
import numpy as np
from jax import lax

PIX = 64
ROTS = 72
SHIFTS = 9
TOP = 8
P_DEV = 16
IMG = 4096
CLASSES = 16
PARTICLES = 512
MOST = 12
N_CLS = 16
N_DP = 2


def draw_references(key, part):
    key_base, key_scale = jax.random.split(jax.random.fold_in(key, 17))
    base_draw = jax.random.normal(key_base, (CLASSES, ROTS, IMG), jnp.float32)
    row_scale = jnp.exp(jax.random.uniform(key_scale, (CLASSES, ROTS, 1), jnp.float32, jnp.log(0.5), jnp.log(2.0)))
    values = jnp.clip(base_draw * row_scale * IMG ** (-0.5), -1.0, 1.0)
    return values.astype(jnp.bfloat16)


def draw_inv_noise(key, part):
    key_base = jax.random.fold_in(jax.random.fold_in(key, 29), 0)
    values = jnp.exp(jax.random.uniform(key_base, (PARTICLES,), jnp.float32, jnp.log(0.5), jnp.log(3.0)))
    return values.astype(jnp.bfloat16)


def level_of(key, shape, shards, least, largest):
    factor_of, own = 1.0, jax.random.fold_in(key, 6)
    for dim, shards_of in shards:
        steps = jnp.exp(jax.random.uniform(jax.random.fold_in(own, dim), (shards_of,), jnp.float32, least / len(shards), largest / len(shards)))
        factor_of = factor_of * jnp.repeat(steps, shape[dim] // shards_of).reshape([-1 if axis == dim else 1 for axis in range(len(shape))])
    return factor_of


def routed_block(key, own, number, rows, count, top, reach, skew):
    order = jax.random.permutation(key, count)
    crowded, usual = portions_of(count, rows * top, reach, skew, True), portions_of(count, rows * top, reach, skew, False)
    places = jnp.arange(count)

    def named(sizes, rotation):
        used = int((sizes > 0).sum())
        fixed = max(1, used // 4)
        passed = fixed + (places - fixed + rotation * (used - fixed)) % max(1, count - fixed)
        return jnp.zeros((count,), jnp.int32).at[order[jnp.where(places < fixed, places, passed)]].set(jnp.asarray(sizes, jnp.int32))

    sizes = jnp.where(number % 4 == 0, named(crowded, number // 4), named(usual, number - number // 4 - 1))
    mixed = jax.random.permutation(jax.random.fold_in(own, 3), count)
    donor, taker = mixed[0:count // 2 * 2:2], mixed[1:count // 2 * 2:2]
    margin = jnp.minimum(sizes[donor] - 1, reach - sizes[taker]) // 2
    margin = jnp.where((donor == order[0]) | (taker == order[0]) | (sizes[taker] == 0), 0, jnp.maximum(margin, 0))
    passed = jax.random.randint(jax.random.fold_in(own, 4), (count // 2,), 0, 1 << 20) % (margin + 1)
    sizes = sizes.at[donor].add(-passed).at[taker].add(passed)
    members = jnp.searchsorted(jnp.cumsum(sizes), jnp.arange(rows * top), side="right").astype(jnp.int32)
    table = members.reshape(top, rows).T
    table = table[jax.random.permutation(jax.random.fold_in(own, 1), rows)]
    rotation = jax.random.randint(jax.random.fold_in(own, 2), (rows, 1), 0, top)
    return jnp.take_along_axis(table, (jnp.arange(top)[None, :] + rotation) % top, axis=1)


def portions_of(count, total, most, slope, full):
    weights = [(1 << 20) // math.isqrt(rank ** slope) + 1 for rank in range(1, count + 1)]
    largest = most if full else min(most, max(-(-total // count), total * weights[0] // sum(weights)))
    least = 1 if total - largest >= count - 1 else 0
    holding, rest = [largest] + [least] * (count - 1), total - largest - least * (count - 1)
    while rest > 0:
        free = [i for i in range(1, count) if holding[i] < largest] or [i for i in range(1, count) if holding[i] < most]
        pool, remaining = sum([weights[i] for i in free]), rest
        for i in free:
            addition = min(most - holding[i], max(1, remaining * weights[i] // pool), rest)
            holding[i] = holding[i] + addition
            rest = rest - addition
    return np.array(holding)


def centred(stream_key, shape, spread, limit, cuts=(), held_as=jnp.bfloat16):
    drawn = jax.random.normal(stream_key, shape, jnp.float32) * spread
    if len(cuts) > 0:
        drawn = level_of(stream_key, shape, cuts, -0.22, 0.18) * drawn
    return jnp.clip(drawn, min=-limit, max=limit).astype(held_as)


def setup_inputs(seed: int = 0) -> dict:
    key_of = jax.random.split(jax.random.key(seed), 5)
    images = centred(key_of[0], (PARTICLES, IMG), 1.0, 6.0, ((0, 32),))
    references = draw_references(jax.random.fold_in(key_of[4], 71), 0)
    candidates_keys = jax.random.split(jax.random.fold_in(key_of[2], 1), PARTICLES // P_DEV)
    candidates_turns = jax.random.permutation(jax.random.fold_in(key_of[2], 3), PARTICLES // P_DEV)
    candidates = jax.vmap(lambda own, number: routed_block(jax.random.fold_in(key_of[2], 2), own, number, P_DEV, CLASSES, TOP, MOST, 2))(candidates_keys, candidates_turns).reshape((PARTICLES, TOP))
    inv_noise = draw_inv_noise(jax.random.fold_in(key_of[4], 71), 0)
    return {"images": images, "references": references, "candidates": candidates, "inv_noise": inv_noise}


OFFSETS = ((0, 0), (1, 0), (-1, 0), (0, 1), (0, -1), (1, 1), (1, -1), (-1, 1), (-1, -1))


def shift_stack(rotated):
    square = rotated.reshape(ROTS, PIX, PIX)
    stacked = jnp.stack([jnp.roll(square, (shift_row, shift_col), axis=(1, 2)) for shift_row, shift_col in OFFSETS], axis=1)
    return stacked.reshape(ROTS * SHIFTS, IMG)


def unshift_sum(summed_back):
    square = summed_back.reshape(ROTS, SHIFTS, PIX, PIX)
    result = jnp.zeros((ROTS, PIX, PIX), jnp.float32)
    for position, offset in enumerate(OFFSETS):
        result = result + jnp.roll(square[:, position], (-offset[0], -offset[1]), axis=(1, 2))
    return result.reshape(ROTS, IMG)


def reference(images, references, candidates, inv_noise):
    capacity = MOST * N_CLS * N_DP
    rows_all = jnp.arange(PARTICLES, dtype=jnp.int32)
    member = jnp.zeros((PARTICLES, CLASSES), jnp.int32).at[rows_all[:, None], candidates].add(1)
    before = jnp.cumsum(member, axis=0) - member
    slot_rank = jnp.take_along_axis(before, candidates, axis=1)
    precision = inv_noise.astype(jnp.float32)

    def entries(class_id):
        in_class = member[:, class_id] > 0
        entry_rows = jnp.nonzero(in_class, size=capacity, fill_value=0)[0].astype(jnp.int32)
        is_live = jnp.arange(capacity, dtype=jnp.int32) < jnp.sum(in_class.astype(jnp.int32))
        return entry_rows, is_live

    def score_class(class_id):
        entry_rows, is_live = entries(class_id)
        entry_images = images[entry_rows]
        rotated = lax.dynamic_index_in_dim(references, class_id, 0, keepdims=False)
        shifted = shift_stack(rotated)
        ref_norms = jnp.sum(jnp.square(rotated.astype(jnp.float32)), axis=1)
        products = lax.dot_general(entry_images, shifted, (((1,), (1,)), ((), ())), preferred_element_type=jnp.float32)
        return precision[entry_rows][:, None] * (products - 0.5 * jnp.repeat(ref_norms, SHIFTS)[None, :])

    scores = lax.map(score_class, jnp.arange(CLASSES, dtype=jnp.int32))
    slot_peak = jnp.max(scores, axis=-1)
    slot_sum = jnp.sum(jnp.exp(scores - slot_peak[..., None]), axis=-1)
    home_peaks = slot_peak[candidates, slot_rank]
    home_sums = slot_sum[candidates, slot_rank]
    row_peak = jnp.max(home_peaks, axis=1)
    norm_total = jnp.sum(home_sums * jnp.exp(home_peaks - row_peak[:, None]), axis=1)

    def back_class(class_id):
        entry_rows, is_live = entries(class_id)
        entry_images = images[entry_rows]
        class_scores = lax.dynamic_index_in_dim(scores, class_id, 0, keepdims=False)
        entry_weights = (jnp.exp(class_scores - row_peak[entry_rows][:, None]) / norm_total[entry_rows][:, None]).astype(jnp.bfloat16)
        entry_weights = jnp.where(is_live[:, None], entry_weights, jnp.zeros_like(entry_weights))
        summed_back = lax.dot_general(entry_weights, entry_images, (((0,), (0,)), ((), ())), preferred_element_type=jnp.float32)
        weight_tot = jnp.sum(entry_weights.astype(jnp.float32), axis=0).reshape(ROTS, SHIFTS).sum(axis=1)
        return unshift_sum(summed_back), weight_tot

    class_sums, class_weights = lax.map(back_class, jnp.arange(CLASSES, dtype=jnp.int32))
    return class_sums, class_weights
```

```python
import functools
import math

import jax
import jax.numpy as jnp
from jax import lax
from jax.experimental import pallas as pl
from jax.experimental.pallas import tpu as pltpu
from jax.sharding import PartitionSpec as P

MESH = pl.DeviceIdType.MESH
LANES = 128
LOW = -1e30

OFFSETS = ((0, 0), (1, 0), (-1, 0), (0, 1), (0, -1), (1, 1), (1, -1), (-1, 1), (-1, -1))


def roll_flat(rows, shift_row, shift_col, side_len):
    result = jnp.roll(rows, shift_row * side_len, axis=1)
    if shift_col != 0:
        column = jnp.arange(side_len * side_len, dtype=jnp.int32) % side_len
        edge = 0 if shift_col > 0 else side_len - 1
        wrapped = jnp.roll(result, shift_col - shift_col * side_len, axis=1)
        plain = jnp.roll(result, shift_col, axis=1)
        result = jnp.where((column == edge)[None, :], wrapped, plain)
    return result


def shift_stack(rotated, side_len):
    return jnp.concatenate(
        [roll_flat(rotated, shift_row, shift_col, side_len) for shift_row, shift_col in OFFSETS],
        axis=0,
    )


def unshift_sum(summed_back, rot_count, side_len):
    square = summed_back.reshape(len(OFFSETS), rot_count, side_len * side_len)
    result = jnp.zeros((rot_count, side_len * side_len), jnp.float32)
    for position, offset in enumerate(OFFSETS):
        result = result + roll_flat(square[position], -offset[0], -offset[1], side_len)
    return result


def on_device(images, references, candidates, inv_noise):
    rows_dev, top_count = candidates.shape
    cls_dev, rot_count, pixels = references.shape
    side_len = math.isqrt(pixels)
    shift_count = len(OFFSETS)
    orient_count = rot_count * shift_count
    n_cls = lax.axis_size("cls")
    classes = cls_dev * n_cls
    slot_depth = max(2, (3 * rows_dev * top_count + 2 * classes - 1) // (2 * classes))
    owner_slots = cls_dev * slot_depth
    slots_all = n_cls * owner_slots
    member = jnp.sum(
        (candidates[:, :, None] == jnp.arange(classes, dtype=jnp.int32)[None, None, :]).astype(
            jnp.int32
        ),
        axis=1,
    )
    earlier = jnp.arange(rows_dev)[:, None] > jnp.arange(rows_dev)[None, :]
    before = jnp.sum(earlier.astype(jnp.int32)[:, :, None] * member[None, :, :], axis=1)
    slot_rank = jnp.take_along_axis(before, candidates, axis=1)
    slot_index = candidates // cls_dev * owner_slots + candidates % cls_dev * slot_depth + slot_rank
    flat_slot = slot_index.reshape(-1)
    source = (
        jnp.full((slots_all,), rows_dev, jnp.int32)
        .at[flat_slot]
        .set(jnp.repeat(jnp.arange(rows_dev, dtype=jnp.int32), top_count))
    )
    images_pad = jnp.concatenate([images, jnp.zeros((1, pixels), jnp.bfloat16)], axis=0)
    noise_pad = jnp.concatenate([inv_noise, jnp.zeros((1,), jnp.bfloat16)], axis=0)
    send_img = images_pad[source].reshape(n_cls, owner_slots * pixels)
    send_noise = noise_pad[source].reshape(n_cls, owner_slots)
    recv_img, recv_noise = (
        lax.all_to_all(send_img, "cls", split_axis=0, concat_axis=0, tiled=True),
        lax.all_to_all(send_noise, "cls", split_axis=0, concat_axis=0, tiled=True),
    )
    live_list = []
    class_pos = 0
    rows_img = recv_img.reshape(n_cls * slot_depth, pixels)
    rows_noise = recv_noise.reshape(-1).astype(jnp.float32)
    shifted = shift_stack(references[class_pos], side_len)
    ref_norms = jnp.sum(jnp.square(references[class_pos].astype(jnp.float32)), axis=1)
    products = lax.dot_general(
        rows_img, shifted, (((1,), (1,)), ((), ())), preferred_element_type=jnp.float32
    )
    class_scores = rows_noise[:, None] * (
        products - 0.5 * jnp.tile(ref_norms, shift_count)[None, :]
    )
    rows_list = [rows_img]
    live_list.append(rows_noise > 0)
    score_list = [class_scores]
    send_scores = jnp.concatenate(
        [part_scores.reshape(n_cls, slot_depth * orient_count) for part_scores in score_list],
        axis=1,
    )
    home_scores = lax.all_to_all(send_scores, "cls", split_axis=0, concat_axis=0, tiled=True)
    own_scores = home_scores.reshape(slots_all, orient_count)[slot_index]
    row_peak = jnp.max(own_scores, axis=(1, 2))
    norm_total = jnp.sum(jnp.exp(own_scores - row_peak[:, None, None]), axis=(1, 2))
    home_weights = (
        jnp.exp(own_scores - row_peak[:, None, None]) / norm_total[:, None, None]
    ).astype(jnp.bfloat16)
    slot_weights = (
        jnp.zeros((slots_all, orient_count), jnp.bfloat16)
        .at[flat_slot]
        .set(home_weights.reshape(-1, orient_count))
    )
    weights = lax.all_to_all(
        slot_weights.reshape(n_cls, owner_slots * orient_count),
        "cls",
        split_axis=0,
        concat_axis=0,
        tiled=True,
    )
    weight_rows = [weights.reshape(n_cls * slot_depth, orient_count)]
    class_pos = 0
    row_weights = weight_rows[class_pos]
    summed_back = lax.dot_general(
        row_weights,
        rows_list[class_pos],
        (((0,), (0,)), ((), ())),
        preferred_element_type=jnp.float32,
    )
    sums_list = [unshift_sum(summed_back, rot_count, side_len)]
    weight_list = [
        jnp.sum(row_weights.astype(jnp.float32), axis=0).reshape(shift_count, rot_count).sum(axis=0)
    ]
    local_sums = jnp.stack(sums_list, axis=0)
    local_weights = jnp.stack(weight_list, axis=0)
    class_sums, class_weights = (
        lax.psum_scatter(local_sums, "dp", scatter_dimension=1, tiled=True),
        lax.psum_scatter(local_weights, "dp", scatter_dimension=1, tiled=True),
    )
    return (class_sums, class_weights)


PLANES = 4
SQUARE = 4


def dense_kernel(
    rows_dev, pixels, half, pad, side, n_cls,
    img_ref, cand_ref, noise_ref, ref_ref, sums_ref, tot_ref,
    held, shifted, norms, expo, peaks, wts, back, mine, stats, stage,
    own_sem, col_send, col_recv, x_send, y_send, a_recv, b_recv, part_send, part_recv,
    st_send, st_recv, out_sem,
):
    cls = lax.axis_index("cls")
    d = lax.axis_index("dp")
    z, y, x = cls // 4, (cls // 2) % 2, cls % 2
    other = 1 - d
    me = cls * 2 + d
    n_dev = n_cls * 2
    width = held.shape[2]
    cut = (width // 2 + LANES - 1) // LANES * LANES
    part_a, part_b = pl.ds(0, cut), pl.ds(cut, width - cut)
    count = len(OFFSETS)
    rows = count * pad
    height = shifted.shape[0]
    tiles = pixels // LANES
    plane_rows = 2 * SQUARE * rows_dev

    def block(bz, by, bx):
        return bz * 4 + by * 2 + bx

    t = z // 2
    order = [z, z + 1 - 2 * (z % 2), 2 - t, 3 - 3 * t]
    x_dev = {"cls": block(z, y, 1 - x), "dp": d}
    y_dev = {"cls": block(z, 1 - y, x), "dp": d}
    up_dev = {"cls": (cls + 4) % n_cls, "dp": d}
    down_dev = {"cls": (cls + n_cls - 4) % n_cls, "dp": d}
    core_dev = {"cls": cls, "dp": other}

    barrier = pltpu.get_barrier_semaphore()

    def greet(dev):
        pl.semaphore_signal(barrier, inc=1, device_id=dev, device_id_type=MESH)

    for dev in (x_dev, y_dev, core_dev):
        greet(dev)
    pl.when(z < PLANES - 1)(lambda: greet(up_dev))
    pl.when(z > 0)(lambda: greet(down_dev))

    def slot(b, core=d):
        return (b // SQUARE) * 2 * SQUARE + core * SQUARE + b % SQUARE

    local = pltpu.make_async_copy(img_ref, held.at[slot(cls), :, pl.ds(0, pixels)], own_sem)
    local.start()

    def describe():
        eye = (
            lax.broadcasted_iota(jnp.int32, (rows_dev, rows_dev), 0)
            == lax.broadcasted_iota(jnp.int32, (rows_dev, rows_dev), 1)
        ).astype(jnp.float32).astype(jnp.bfloat16)
        dims = (((1,), (1,)), ((), ()))
        names = lax.dot_general(
            eye, cand_ref[...].astype(jnp.float32).astype(jnp.bfloat16), dims, preferred_element_type=jnp.float32
        )
        noise = jnp.broadcast_to(noise_ref[...].astype(jnp.float32), (8, rows_dev)).astype(jnp.bfloat16)
        level = lax.dot_general(eye, noise, dims, preferred_element_type=jnp.float32)[:, 0:1]
        lanes = lax.broadcasted_iota(jnp.int32, (rows_dev, LANES), 1).astype(jnp.float32)
        named = names[:, 0:1] == lanes
        for k in range(1, cand_ref.shape[0]):
            named = jnp.logical_or(named, names[:, k:k + 1] == lanes)
        held[slot(cls), :, pixels:pixels + LANES] = jnp.where(named, level, 0.0).astype(jnp.bfloat16)

    describe()
    local.wait()

    lane8 = lax.broadcasted_iota(jnp.int32, (8, LANES), 1)
    upper = lane8 >= side

    def turn(v, dx):
        if dx == 0:
            return v
        source = lane8 // side * side + (lane8 + dx + side) % side
        return jnp.take_along_axis(v, source, axis=1)

    def swap(v):
        return pltpu.roll(v, side, 1)

    def at(j):
        return pl.ds(pl.multiple_of(j * LANES, LANES), LANES)

    def pick_rows():
        row = lax.broadcasted_iota(jnp.int32, (pad, 2 * half), 0)
        col = lax.broadcasted_iota(jnp.int32, (pad, 2 * half), 1)
        pick = jnp.logical_and(col == row + d * half, row < half).astype(jnp.float32).astype(jnp.bfloat16)
        width_c = pixels // 8
        for c in range(8):
            cols = pl.ds(c * width_c, width_c)
            back[0:pad, cols] = jnp.dot(pick, ref_ref[0, :, cols], preferred_element_type=jnp.float32)
        norms[...] = jnp.broadcast_to(
            jnp.sum(jnp.square(back[0:pad, :]), axis=1, keepdims=True), norms.shape
        )

    def build():
        def column(j, carry):
            before, after = (j + tiles - 1) % tiles, (j + 1) % tiles
            parts = []
            for dy, dx in OFFSETS:
                for i in range(pad // 8):
                    rs = pl.ds(8 * i, 8)
                    if dy == 0:
                        v = back[rs, at(j)]
                    elif dy == 1:
                        v = swap(jnp.where(upper, back[rs, at(before)], back[rs, at(j)]))
                    else:
                        v = swap(jnp.where(upper, back[rs, at(j)], back[rs, at(after)]))
                    parts.append(turn(v, -dx))
            while len(parts) * 8 < height:
                parts.append(jnp.zeros((8, LANES), jnp.float32))
            for q in range(0, len(parts), 2):
                shifted[8 * q:8 * q + 16, at(j)] = jnp.concatenate(parts[q:q + 2], axis=0).astype(jnp.bfloat16)
            return carry

        lax.fori_loop(0, tiles, column, 0)

    pick_rows()
    build()
    lines = 5 - jnp.where(z == 0, 1, 0) - jnp.where(z == PLANES - 1, 1, 0)
    pl.semaphore_wait(barrier, lines)

    def remote(src, dst, send, recv, dev):
        return pltpu.make_async_remote_copy(
            src_ref=src, dst_ref=dst, send_sem=send, recv_sem=recv, device_id=dev, device_id_type=MESH
        )

    pieces = (part_a, part_b)

    def full(k, h, which, b, dev):
        ref = held.at[slot(b), :, pieces[h]]
        return remote(ref, ref, col_send.at[k, h, which], col_recv.at[h, b], dev)

    def arrived(h, b, dev):
        ref = held.at[slot(b), :, pieces[h]]
        remote(ref, ref, col_send.at[0, h, 0], col_recv.at[h, b], dev).wait_recv()

    def to_core(index, b):
        ref = held.at[slot(b)]
        return remote(ref, ref, part_send.at[index], part_recv.at[b], core_dev)

    def piece(b, cols, send, recv, dev):
        ref = held.at[slot(b), :, cols]
        return remote(ref, ref, send, recv.at[b], dev)

    started = []

    def go(copy, cond=None):
        started.append((copy, cond))
        if cond is None:
            copy.start()
        else:
            pl.when(cond)(lambda: copy.start())

    def column_sends(k, h):
        b = block(order[k], y, x)
        zk = order[k]
        if k == 0:
            up, down = z < PLANES - 1, z > 0
        else:
            up = jnp.logical_and(zk < z, z < PLANES - 1)
            down = jnp.logical_and(zk > z, z > 0)
        go(full(k, h, 2, b, up_dev), up)
        go(full(k, h, 3, b, down_dev), down)
        go(full(k, h, 0, b, x_dev))
        go(full(k, h, 1, b, y_dev))
        if h == 1:
            go(to_core(k, b))

    def wait_core(b):
        ref = held.at[slot(b, other)]
        remote(ref, ref, part_send.at[0], part_recv.at[b], core_dev).wait_recv()

    depth = pixels // 4

    def chunk_cols(c):
        return pl.ds(pl.multiple_of(c * depth, depth), depth)

    one = (lax.broadcasted_iota(jnp.int32, (8, LANES), 1) == cls).astype(jnp.float32).astype(jnp.bfloat16)

    def score(plane):
        first = plane * 2 * SQUARE

        def part(c, acc):
            cols = chunk_cols(c)
            right = held[pl.ds(first, 2 * SQUARE), :, cols].reshape(plane_rows, depth)
            return acc + lax.dot_general(
                shifted[:, cols], right, (((1,), (1,)), ((), ())), preferred_element_type=jnp.float32
            )

        prod = lax.fori_loop(0, 4, part, jnp.zeros((height, plane_rows), jnp.float32))
        meta = held[pl.ds(first, 2 * SQUARE), :, pixels:pixels + LANES].reshape(plane_rows, LANES)
        noise = lax.dot_general(one, meta, (((1,), (1,)), ((), ())), preferred_element_type=jnp.float32)[0:1, :]
        prod = prod[0:rows].reshape(count, pad, plane_rows)
        offset = 0.5 * norms[:, 0:1]
        valid = jnp.logical_and(
            noise[None] > 0,
            lax.broadcasted_iota(jnp.int32, (1, pad, plane_rows), 1) < half,
        )
        value = jnp.where(valid, noise[None] * (prod - offset[None]), LOW)
        peak = jnp.max(jnp.max(value, axis=0), axis=0, keepdims=True)
        grown = jnp.where(valid, jnp.exp(value - peak[None]), 0.0)
        total = jnp.sum(jnp.sum(grown, axis=0), axis=0, keepdims=True)
        peaks[plane, 0:1, :] = peak
        peaks[plane, 1:2, :] = total
        expo[plane] = grown.reshape(rows, plane_rows)

    pairs = ((1, 2), (0, 3))

    def stat(m, j):
        t = (me + j) % n_dev
        return remote(mine.at[m], stats.at[m, me], st_send.at[m], st_recv.at[m], {"cls": t // 2, "dp": t % 2})

    def send_stats(m):
        for g, plane in enumerate(pairs[m]):
            mine[m, :, g * plane_rows:(g + 1) * plane_rows] = peaks[plane]
        stats[m, me] = mine[m]

        def send(j, carry):
            stat(m, j).start()
            return carry

        lax.fori_loop(1, n_dev, send, 0)

    def all_of(m, sem):
        ref = stats.at[m, pl.ds(0, n_dev - 1)]
        return pltpu.make_async_copy(ref, ref, sem.at[m])

    def weigh(m):
        all_of(m, st_recv).wait()
        every = stats[m]
        top = jnp.max(every[:, 0:1, :], axis=0)
        norm = jnp.sum(every[:, 1:2, :] * jnp.exp(every[:, 0:1, :] - top[None]), axis=0)
        factor = jnp.exp(mine[m, 0:1, :] - top) / norm
        flat = jnp.zeros((pad, plane_rows), jnp.float32)
        for g, plane in enumerate(pairs[m]):
            weight = expo[plane] * factor[:, g * plane_rows:(g + 1) * plane_rows]
            if height > rows:
                weight = jnp.concatenate([weight, jnp.zeros((height - rows, plane_rows), jnp.float32)], axis=0)
            weight = weight.astype(jnp.bfloat16)
            wts[m, :, g * plane_rows:(g + 1) * plane_rows] = weight
            flat = flat + jnp.sum(weight[0:rows].astype(jnp.float32).reshape(count, pad, plane_rows), axis=0)
        return flat

    def project(m):
        def part(c, carry):
            cols = chunk_cols(c)
            right = jnp.concatenate(
                [
                    held[plane * 2 * SQUARE:(plane + 1) * 2 * SQUARE, :, cols].reshape(plane_rows, depth)
                    for plane in pairs[m]
                ],
                axis=0,
            )
            value = jnp.dot(wts[m], right, preferred_element_type=jnp.float32)
            back[:, cols] = value if m == 0 else back[:, cols] + value
            return carry

        lax.fori_loop(0, 4, part, 0)

    def core_in(k):
        for by in (0, 1):
            for bx in (0, 1):
                wait_core(block(order[k], by, bx))

    def diagonal(k):
        b = block(order[k], 1 - y, 1 - x)
        piece(b, part_a, y_send.at[k], a_recv, x_dev).wait_recv()
        piece(b, part_b, x_send.at[k], b_recv, y_dev).wait_recv()
        go(to_core(3 * PLANES + k, b))

    column_sends(0, 0)
    column_sends(0, 1)
    for k in range(PLANES):
        xb = block(order[k], y, 1 - x)
        yb = block(order[k], 1 - y, x)
        for h in range(2):
            if k + 1 < PLANES:
                arrived(h, block(order[k + 1], y, x), up_dev)
                column_sends(k + 1, h)
            arrived(h, xb, x_dev)
            if h == 1:
                go(piece(xb, part_b, x_send.at[k], b_recv, y_dev))
                go(to_core(PLANES + k, xb))
            arrived(h, yb, y_dev)
            if h == 0:
                go(piece(yb, part_a, y_send.at[k], a_recv, x_dev))
            else:
                go(to_core(2 * PLANES + k, yb))
        if k >= 1:
            diagonal(k - 1)
        if k >= 2:
            core_in(k - 2)
            score(order[k - 2])
    core_in(2)
    score(order[2])
    send_stats(0)
    diagonal(3)
    core_in(3)
    score(order[3])
    send_stats(1)
    flat = weigh(0)
    project(0)
    flat = flat + weigh(1)
    project(1)

    place = {offset: i for i, offset in enumerate(OFFSETS)}

    def finish(j, carry):
        before, after = (j + tiles - 1) % tiles, (j + 1) % tiles
        for i in range(pad // 8):
            keep = min(8, half - 8 * i)

            def part(dy, dx, jj):
                return back[pl.ds(place[(dy, dx)] * pad + 8 * i, 8), at(jj)]

            value = None
            for dx in (0, 1, -1):
                edge = jnp.where(
                    upper,
                    part(1, dx, j) + part(-1, dx, before),
                    part(1, dx, after) + part(-1, dx, j),
                )
                term = turn(part(0, dx, j) + swap(edge), dx)
                value = term if value is None else value + term
            stage[pl.ds(8 * i * tiles + j, 8, stride=tiles), :] = value
        return carry

    lax.fori_loop(0, tiles, finish, 0)
    out = pltpu.make_async_copy(stage.at[pl.ds(0, half * tiles)], sums_ref, out_sem)
    out.start()
    column = jnp.sum(flat, axis=1, keepdims=True)
    eye = lax.broadcasted_iota(jnp.int32, (pad, LANES), 0) == lax.broadcasted_iota(jnp.int32, (pad, LANES), 1)
    tot_ref[...] = jnp.sum(jnp.where(eye, column, 0.0), axis=0, keepdims=True)[:, 0:half]
    for copy, cond in started:
        if cond is None:
            copy.wait_send()
        else:
            pl.when(cond)(lambda copy=copy: copy.wait_send())
    for m in range(2):
        all_of(m, st_send).wait()
    out.wait()


def dense_on_device(images, references, candidates, inv_noise):
    rows_dev, pixels = images.shape
    n_cls, n_dp = lax.axis_size("cls"), lax.axis_size("dp")
    rot_count = references.shape[1]
    half = rot_count // n_dp
    pad = (half + 7) // 8 * 8
    side = math.isqrt(pixels)
    height = (len(OFFSETS) * pad + 15) // 16 * 16
    plane_rows = 2 * SQUARE * rows_dev
    tiles = pixels // LANES
    width = pixels + LANES
    dma = pltpu.SemaphoreType.DMA
    vmem = pl.BlockSpec(memory_space=pltpu.VMEM)
    hbm = pl.BlockSpec(memory_space=pl.ANY)
    sums, totals = pl.pallas_call(
        functools.partial(dense_kernel, rows_dev, pixels, half, pad, side, n_cls),
        out_shape=(
            jax.ShapeDtypeStruct((half * tiles, LANES), jnp.float32),
            jax.ShapeDtypeStruct((1, half), jnp.float32),
        ),
        in_specs=[hbm, vmem, vmem, vmem],
        out_specs=(hbm, vmem),
        scratch_shapes=[
            pltpu.VMEM((n_cls * n_dp, rows_dev, width), jnp.bfloat16),
            pltpu.VMEM((height, pixels), jnp.bfloat16),
            pltpu.VMEM((pad, LANES), jnp.float32),
            pltpu.VMEM((PLANES, len(OFFSETS) * pad, plane_rows), jnp.float32),
            pltpu.VMEM((PLANES, 2, plane_rows), jnp.float32),
            pltpu.VMEM((2, height, 2 * plane_rows), jnp.bfloat16),
            pltpu.VMEM((height, pixels), jnp.float32),
            pltpu.VMEM((2, 2, 2 * plane_rows), jnp.float32),
            pltpu.VMEM((2, n_cls * n_dp, 2, 2 * plane_rows), jnp.float32),
            pltpu.VMEM((pad * tiles, LANES), jnp.float32),
            dma,
            dma((PLANES, 2, 4)),
            dma((2, n_cls)),
            dma((PLANES,)),
            dma((PLANES,)),
            dma((n_cls,)),
            dma((n_cls,)),
            dma((4 * PLANES,)),
            dma((n_cls,)),
            dma((2,)),
            dma((2,)),
            dma,
        ],
        compiler_params=pltpu.CompilerParams(
            collective_id=0, has_side_effects=True, vmem_limit_bytes=56 << 20
        ),
    )(images, candidates.T, inv_noise.reshape(1, rows_dev), references)
    return sums.reshape(1, half, pixels), totals


def solution(mesh):
    placed = (
        P(("cls", "dp"), None),
        P("cls", None, None),
        P(("cls", "dp"), None),
        P(("cls", "dp")),
    )
    n_cls, n_dp = mesh.shape["cls"], mesh.shape["dp"]
    dense = n_cls == PLANES * SQUARE and n_dp == 2
    return jax.shard_map(
        dense_on_device if dense else on_device,
        mesh=mesh,
        in_specs=placed,
        out_specs=(P("cls", "dp", None), P("cls", "dp")),
        check_vma=False,
    )
```

```python
import functools
import math

import jax
import jax.numpy as jnp
from jax import lax
from jax.experimental import pallas as pl
from jax.experimental.pallas import tpu as pltpu
from jax.sharding import PartitionSpec as P

MESH = pl.DeviceIdType.MESH
LANES = 128
LOW = -1e30

OFFSETS = ((0, 0), (1, 0), (-1, 0), (0, 1), (0, -1), (1, 1), (1, -1), (-1, 1), (-1, -1))


def roll_flat(rows, shift_row, shift_col, side_len):
    result = jnp.roll(rows, shift_row * side_len, axis=1)
    if shift_col != 0:
        column = jnp.arange(side_len * side_len, dtype=jnp.int32) % side_len
        edge = 0 if shift_col > 0 else side_len - 1
        wrapped = jnp.roll(result, shift_col - shift_col * side_len, axis=1)
        plain = jnp.roll(result, shift_col, axis=1)
        result = jnp.where((column == edge)[None, :], wrapped, plain)
    return result


def shift_stack(rotated, side_len):
    return jnp.concatenate(
        [roll_flat(rotated, shift_row, shift_col, side_len) for shift_row, shift_col in OFFSETS],
        axis=0,
    )


def unshift_sum(summed_back, rot_count, side_len):
    square = summed_back.reshape(len(OFFSETS), rot_count, side_len * side_len)
    result = jnp.zeros((rot_count, side_len * side_len), jnp.float32)
    for position, offset in enumerate(OFFSETS):
        result = result + roll_flat(square[position], -offset[0], -offset[1], side_len)
    return result


def on_device(images, references, candidates, inv_noise):
    rows_dev, top_count = candidates.shape
    cls_dev, rot_count, pixels = references.shape
    side_len = math.isqrt(pixels)
    shift_count = len(OFFSETS)
    orient_count = rot_count * shift_count
    n_cls = lax.axis_size("cls")
    classes = cls_dev * n_cls
    slot_depth = max(2, (3 * rows_dev * top_count + 2 * classes - 1) // (2 * classes))
    owner_slots = cls_dev * slot_depth
    slots_all = n_cls * owner_slots
    member = jnp.sum(
        (candidates[:, :, None] == jnp.arange(classes, dtype=jnp.int32)[None, None, :]).astype(
            jnp.int32
        ),
        axis=1,
    )
    earlier = jnp.arange(rows_dev)[:, None] > jnp.arange(rows_dev)[None, :]
    before = jnp.sum(earlier.astype(jnp.int32)[:, :, None] * member[None, :, :], axis=1)
    slot_rank = jnp.take_along_axis(before, candidates, axis=1)
    slot_index = candidates // cls_dev * owner_slots + candidates % cls_dev * slot_depth + slot_rank
    flat_slot = slot_index.reshape(-1)
    source = (
        jnp.full((slots_all,), rows_dev, jnp.int32)
        .at[flat_slot]
        .set(jnp.repeat(jnp.arange(rows_dev, dtype=jnp.int32), top_count))
    )
    images_pad = jnp.concatenate([images, jnp.zeros((1, pixels), jnp.bfloat16)], axis=0)
    noise_pad = jnp.concatenate([inv_noise, jnp.zeros((1,), jnp.bfloat16)], axis=0)
    send_img = images_pad[source].reshape(n_cls, owner_slots * pixels)
    send_noise = noise_pad[source].reshape(n_cls, owner_slots)
    recv_img, recv_noise = (
        lax.all_to_all(send_img, "cls", split_axis=0, concat_axis=0, tiled=True),
        lax.all_to_all(send_noise, "cls", split_axis=0, concat_axis=0, tiled=True),
    )
    live_list = []
    class_pos = 0
    rows_img = recv_img.reshape(n_cls * slot_depth, pixels)
    rows_noise = recv_noise.reshape(-1).astype(jnp.float32)
    shifted = shift_stack(references[class_pos], side_len)
    ref_norms = jnp.sum(jnp.square(references[class_pos].astype(jnp.float32)), axis=1)
    products = lax.dot_general(
        rows_img, shifted, (((1,), (1,)), ((), ())), preferred_element_type=jnp.float32
    )
    class_scores = rows_noise[:, None] * (
        products - 0.5 * jnp.tile(ref_norms, shift_count)[None, :]
    )
    rows_list = [rows_img]
    live_list.append(rows_noise > 0)
    score_list = [class_scores]
    send_scores = jnp.concatenate(
        [part_scores.reshape(n_cls, slot_depth * orient_count) for part_scores in score_list],
        axis=1,
    )
    home_scores = lax.all_to_all(send_scores, "cls", split_axis=0, concat_axis=0, tiled=True)
    own_scores = home_scores.reshape(slots_all, orient_count)[slot_index]
    row_peak = jnp.max(own_scores, axis=(1, 2))
    norm_total = jnp.sum(jnp.exp(own_scores - row_peak[:, None, None]), axis=(1, 2))
    home_weights = (
        jnp.exp(own_scores - row_peak[:, None, None]) / norm_total[:, None, None]
    ).astype(jnp.bfloat16)
    slot_weights = (
        jnp.zeros((slots_all, orient_count), jnp.bfloat16)
        .at[flat_slot]
        .set(home_weights.reshape(-1, orient_count))
    )
    weights = lax.all_to_all(
        slot_weights.reshape(n_cls, owner_slots * orient_count),
        "cls",
        split_axis=0,
        concat_axis=0,
        tiled=True,
    )
    weight_rows = [weights.reshape(n_cls * slot_depth, orient_count)]
    class_pos = 0
    row_weights = weight_rows[class_pos]
    summed_back = lax.dot_general(
        row_weights,
        rows_list[class_pos],
        (((0,), (0,)), ((), ())),
        preferred_element_type=jnp.float32,
    )
    sums_list = [unshift_sum(summed_back, rot_count, side_len)]
    weight_list = [
        jnp.sum(row_weights.astype(jnp.float32), axis=0).reshape(shift_count, rot_count).sum(axis=0)
    ]
    local_sums = jnp.stack(sums_list, axis=0)
    local_weights = jnp.stack(weight_list, axis=0)
    class_sums, class_weights = (
        lax.psum_scatter(local_sums, "dp", scatter_dimension=1, tiled=True),
        lax.psum_scatter(local_weights, "dp", scatter_dimension=1, tiled=True),
    )
    return (class_sums, class_weights)


PLANES = 4
SQUARE = 4
BIG = 1e30


def dense_kernel(
    rows_dev, pixels, half, pad, side, n_cls,
    img_ref, cand_ref, noise_ref, ref_ref, sums_ref, tot_ref,
    held, shifted, turned, offset, acc, expo, peaks, wts, back, mine, stats,
    own_sem, col_send, col_recv, x_send, y_send, a_recv, b_recv, part_send, part_recv,
    st_send, st_recv,
):
    cls = lax.axis_index("cls")
    d = lax.axis_index("dp")
    z, y, x = cls // 4, (cls // 2) % 2, cls % 2
    other = 1 - d
    me = cls * 2 + d
    n_dev = n_cls * 2
    width = held.shape[2]
    cut = (width // 2 + LANES - 1) // LANES * LANES
    part_a, part_b = pl.ds(0, cut), pl.ds(cut, width - cut)
    band = shifted.shape[0] // 3
    tiles = pixels // LANES
    plane_rows = 2 * SQUARE * rows_dev

    def block(bz, by, bx):
        return bz * 4 + by * 2 + bx

    t = z // 2
    order = [z, z + 1 - 2 * (z % 2), 2 - t, 3 - 3 * t]
    x_dev = {"cls": block(z, y, 1 - x), "dp": d}
    y_dev = {"cls": block(z, 1 - y, x), "dp": d}
    up_dev = {"cls": (cls + 4) % n_cls, "dp": d}
    down_dev = {"cls": (cls + n_cls - 4) % n_cls, "dp": d}
    core_dev = {"cls": cls, "dp": other}

    barrier = pltpu.get_barrier_semaphore()

    def greet(dev):
        pl.semaphore_signal(barrier, inc=1, device_id=dev, device_id_type=MESH)

    for dev in (x_dev, y_dev, core_dev):
        greet(dev)
    pl.when(z < PLANES - 1)(lambda: greet(up_dev))
    pl.when(z > 0)(lambda: greet(down_dev))

    def slot(b, core=d):
        return (b // SQUARE) * 2 * SQUARE + core * SQUARE + b % SQUARE

    local = pltpu.make_async_copy(img_ref, held.at[slot(cls), :, pl.ds(0, pixels)], own_sem)
    local.start()

    def describe():
        eye = (
            lax.broadcasted_iota(jnp.int32, (rows_dev, rows_dev), 0)
            == lax.broadcasted_iota(jnp.int32, (rows_dev, rows_dev), 1)
        ).astype(jnp.float32).astype(jnp.bfloat16)
        dims = (((1,), (1,)), ((), ()))
        names = lax.dot_general(
            eye, cand_ref[...].astype(jnp.float32).astype(jnp.bfloat16), dims, preferred_element_type=jnp.float32
        )
        noise = jnp.broadcast_to(noise_ref[...].astype(jnp.float32), (8, rows_dev)).astype(jnp.bfloat16)
        level = lax.dot_general(eye, noise, dims, preferred_element_type=jnp.float32)[:, 0:1]
        lanes = lax.broadcasted_iota(jnp.int32, (rows_dev, LANES), 1).astype(jnp.float32)
        named = names[:, 0:1] == lanes
        for k in range(1, cand_ref.shape[0]):
            named = jnp.logical_or(named, names[:, k:k + 1] == lanes)
        held[slot(cls), :, pixels:pixels + LANES] = jnp.where(named, level, 0.0).astype(jnp.bfloat16)

    describe()
    local.wait()

    def moves(first, second):
        row = lax.broadcasted_iota(jnp.int32, (LANES, 2 * LANES), 0)
        col = lax.broadcasted_iota(jnp.int32, (LANES, 2 * LANES), 1)
        step = jnp.where(col < LANES, first, second)
        source = jnp.bitwise_or(jnp.bitwise_and(col, side), jnp.bitwise_and(col + step, side - 1))
        return (row == source).astype(jnp.float32).astype(jnp.bfloat16)

    def left(v):
        return jnp.concatenate([v[:, LANES:], v[:, :LANES]], axis=1)

    def build():
        row = lax.broadcasted_iota(jnp.int32, (pad, 2 * half), 0)
        col = lax.broadcasted_iota(jnp.int32, (pad, 2 * half), 1)
        pick = jnp.logical_and(col == row + d * half, row < half).astype(jnp.float32).astype(jnp.bfloat16)
        width_c = pixels // 8
        for c in range(8):
            cols = pl.ds(c * width_c, width_c)
            back[0:pad, cols] = jnp.dot(pick, ref_ref[0, :, cols], preferred_element_type=jnp.float32)
        for i in range(pad // 8):
            v = back[8 * i:8 * i + 8, :]
            back[pad + 8 * i:pad + 8 * i + 8, :] = pltpu.roll(v, side, 1)
            back[2 * pad + 8 * i:2 * pad + 8 * i + 8, :] = pltpu.roll(v, pixels - side, 1)
        if band > 3 * pad:
            back[3 * pad:band, :] = jnp.zeros((band - 3 * pad, pixels), jnp.float32)
        energy = 0.5 * jnp.sum(jnp.square(back[0:pad, :]), axis=1, keepdims=True)
        spare = lax.broadcasted_iota(jnp.int32, (pad, 1), 0) >= half
        energy = jnp.where(spare, BIG, energy)
        for dy in range(3):
            offset[dy * pad:(dy + 1) * pad, :] = jnp.broadcast_to(energy, (pad, LANES))
        if band > 3 * pad:
            offset[3 * pad:band, :] = jnp.full((band - 3 * pad, LANES), BIG, jnp.float32)
        both = moves(-1, 1)
        for j in range(tiles):
            cols = pl.ds(j * LANES, LANES)
            base = back[:, cols].astype(jnp.bfloat16)
            pair = jnp.dot(base, both, preferred_element_type=jnp.float32).astype(jnp.bfloat16)
            shifted[0:band, cols] = base
            shifted[band:2 * band, cols] = pair[:, 0:LANES]
            shifted[2 * band:3 * band, cols] = pair[:, LANES:2 * LANES]

    build()
    lines = 5 - jnp.where(z == 0, 1, 0) - jnp.where(z == PLANES - 1, 1, 0)
    pl.semaphore_wait(barrier, lines)

    def remote(src, dst, send, recv, dev):
        return pltpu.make_async_remote_copy(
            src_ref=src, dst_ref=dst, send_sem=send, recv_sem=recv, device_id=dev, device_id_type=MESH
        )

    pieces = (part_a, part_b)

    def full(k, h, which, b, dev):
        ref = held.at[slot(b), :, pieces[h]]
        return remote(ref, ref, col_send.at[k, h, which], col_recv.at[h, b], dev)

    def arrived(h, b, dev):
        ref = held.at[slot(b), :, pieces[h]]
        remote(ref, ref, col_send.at[0, h, 0], col_recv.at[h, b], dev).wait_recv()

    def to_core(index, b):
        ref = held.at[slot(b)]
        return remote(ref, ref, part_send.at[index], part_recv.at[b], core_dev)

    def piece(b, cols, send, recv, dev):
        ref = held.at[slot(b), :, cols]
        return remote(ref, ref, send, recv.at[b], dev)

    started = []

    def go(copy, cond=None):
        started.append((copy, cond))
        if cond is None:
            copy.start()
        else:
            pl.when(cond)(lambda: copy.start())

    def column_sends(k, h):
        b = block(order[k], y, x)
        zk = order[k]
        if k == 0:
            up, down = z < PLANES - 1, z > 0
        else:
            up = jnp.logical_and(zk < z, z < PLANES - 1)
            down = jnp.logical_and(zk > z, z > 0)
        go(full(k, h, 2, b, up_dev), up)
        go(full(k, h, 3, b, down_dev), down)
        go(full(k, h, 0, b, x_dev))
        go(full(k, h, 1, b, y_dev))
        if h == 1:
            go(to_core(k, b))

    def wait_core(b):
        ref = held.at[slot(b, other)]
        remote(ref, ref, part_send.at[0], part_recv.at[b], core_dev).wait_recv()

    depth = pixels // 4

    def chunk_cols(c):
        return pl.ds(pl.multiple_of(c * depth, depth), depth)

    one = (lax.broadcasted_iota(jnp.int32, (8, LANES), 1) == cls).astype(jnp.float32).astype(jnp.bfloat16)

    def multiply(plane, c):
        first = plane * 2 * SQUARE
        cols = pl.ds(c * depth, depth)
        right = held[pl.ds(first, 2 * SQUARE), :, cols].reshape(plane_rows, depth)
        value = lax.dot_general(
            shifted[:, cols], right, (((1,), (1,)), ((), ())), preferred_element_type=jnp.float32
        )
        acc[...] = value if c == 0 else acc[...] + value

    def score(plane):
        prod = acc[...]
        first = plane * 2 * SQUARE
        meta = held[pl.ds(first, 2 * SQUARE), :, pixels:pixels + LANES].reshape(plane_rows, LANES)
        noise = lax.dot_general(one, meta, (((1,), (1,)), ((), ())), preferred_element_type=jnp.float32)[0:1, :]
        live = noise > 0
        value = noise[None] * (prod.reshape(3, band, plane_rows) - offset[...][None])
        peak = jnp.max(jnp.max(value, axis=0), axis=0, keepdims=True)
        peak = jnp.where(live, peak, LOW)
        grown = jnp.where(live[None], jnp.exp(value - peak[None]), 0.0)
        total = jnp.sum(jnp.sum(grown, axis=0), axis=0, keepdims=True)
        peaks[plane, 0:1, :] = peak
        peaks[plane, 1:2, :] = total
        expo[plane] = grown

    both = moves(1, -1)

    def turn(plane, c):
        first = plane * 2 * SQUARE
        spans = [pl.ds((c * 4 + u) * LANES, LANES) for u in range(4)]
        source = jnp.concatenate(
            [held[pl.ds(first, 2 * SQUARE), :, cols].reshape(plane_rows, LANES) for cols in spans], axis=0
        )
        pair = jnp.dot(source, both, preferred_element_type=jnp.float32).astype(jnp.bfloat16)
        for u, cols in enumerate(spans):
            turned[0, plane, :, cols] = pair[u * plane_rows:(u + 1) * plane_rows, 0:LANES]
            turned[1, plane, :, cols] = pair[u * plane_rows:(u + 1) * plane_rows, LANES:2 * LANES]

    pairs = ((1, 2), (0, 3))

    def stat(m, j):
        t = (me + j) % n_dev
        return remote(mine.at[m], stats.at[m, me], st_send.at[m], st_recv.at[m], {"cls": t // 2, "dp": t % 2})

    def send_stats(m):
        for g, plane in enumerate(pairs[m]):
            mine[m, :, g * plane_rows:(g + 1) * plane_rows] = peaks[plane]
        stats[m, me] = mine[m]

        def send(j, carry):
            stat(m, j).start()
            return carry

        lax.fori_loop(1, n_dev, send, 0)

    def all_of(m, sem):
        ref = stats.at[m, pl.ds(0, n_dev - 1)]
        return pltpu.make_async_copy(ref, ref, sem.at[m])

    def weigh(m):
        all_of(m, st_recv).wait()
        every = stats[m]
        top = jnp.max(every[:, 0:1, :], axis=0)
        norm = jnp.sum(every[:, 1:2, :] * jnp.exp(every[:, 0:1, :] - top[None]), axis=0)
        factor = jnp.exp(mine[m, 0:1, :] - top) / norm
        flat = jnp.zeros((band, plane_rows), jnp.float32)
        for g, plane in enumerate(pairs[m]):
            weight = (expo[plane] * factor[None, :, g * plane_rows:(g + 1) * plane_rows]).astype(jnp.bfloat16)
            for dx in range(3):
                base = (2 * dx + g) * plane_rows
                wts[m, :, base:base + plane_rows] = weight[dx]
            flat = flat + jnp.sum(weight.astype(jnp.float32), axis=0)
        return sum(flat[dy * pad:(dy + 1) * pad] for dy in range(3))

    def project(m):
        def part(c, carry):
            cols = pl.ds(c * depth, depth)
            right = jnp.concatenate(
                [
                    held[plane * 2 * SQUARE:(plane + 1) * 2 * SQUARE, :, cols].reshape(plane_rows, depth)
                    for plane in pairs[m]
                ]
                + [turned[side_of, plane, :, cols] for side_of in range(2) for plane in pairs[m]],
                axis=0,
            )
            value = jnp.dot(wts[m], right, preferred_element_type=jnp.float32)
            back[:, cols] = value if m == 0 else back[:, cols] + value
            return carry

        for c in range(4):
            part(c, 0)

    def core_in(k):
        for by in (0, 1):
            for bx in (0, 1):
                wait_core(block(order[k], by, bx))

    def diagonal(k):
        b = block(order[k], 1 - y, 1 - x)
        piece(b, part_a, y_send.at[k], a_recv, x_dev).wait_recv()
        piece(b, part_b, x_send.at[k], b_recv, y_dev).wait_recv()
        go(to_core(3 * PLANES + k, b))

    work = []

    def queue_score(k):
        work.append(lambda: (core_in(k), multiply(order[k], 0), multiply(order[k], 1)))
        work.append(lambda: (multiply(order[k], 2), multiply(order[k], 3), score(order[k])))

    def queue_turn(k):
        for c in range(0, tiles // 4, 2):
            work.append(lambda c=c: (turn(order[k], c), turn(order[k], c + 1)))

    def idle():
        if work:
            work.pop(0)()

    def drain():
        while work:
            idle()

    column_sends(0, 0)
    column_sends(0, 1)
    for k in range(PLANES):
        xb = block(order[k], y, 1 - x)
        yb = block(order[k], 1 - y, x)
        for h in range(2):
            if k + 1 < PLANES:
                arrived(h, block(order[k + 1], y, x), up_dev)
                column_sends(k + 1, h)
            idle()
            arrived(h, xb, x_dev)
            if h == 1:
                go(piece(xb, part_b, x_send.at[k], b_recv, y_dev))
                go(to_core(PLANES + k, xb))
            idle()
            arrived(h, yb, y_dev)
            if h == 0:
                go(piece(yb, part_a, y_send.at[k], a_recv, x_dev))
            else:
                go(to_core(2 * PLANES + k, yb))
            idle()
        if k >= 1:
            diagonal(k - 1)
            queue_score(k - 1)
            queue_turn(k - 1)
    idle()
    idle()
    send_stats(0)
    diagonal(3)
    drain()
    queue_score(3)
    drain()
    send_stats(1)
    queue_turn(3)
    drain()
    flat = weigh(0)
    project(0)
    flat = flat + weigh(1)
    project(1)

    for i in range(pad // 8):
        above, same, below = (back[k * pad + 8 * i:k * pad + 8 * i + 8, :] for k in (1, 0, 2))
        value = same + pltpu.roll(left(above) + below, side, 1)
        for j in range(tiles):
            sums_ref[pl.ds(8 * i * tiles + j, 8, stride=tiles), :] = value[:, j * LANES:(j + 1) * LANES]
    column = jnp.sum(flat, axis=1, keepdims=True)
    eye = lax.broadcasted_iota(jnp.int32, (pad, LANES), 0) == lax.broadcasted_iota(jnp.int32, (pad, LANES), 1)
    tot_ref[...] = jnp.sum(jnp.where(eye, column, 0.0), axis=0, keepdims=True)[:, 0:half]
    for copy, cond in started:
        if cond is None:
            copy.wait_send()
        else:
            pl.when(cond)(lambda copy=copy: copy.wait_send())
    for m in range(2):
        all_of(m, st_send).wait()


def deliver(rows, sums_ref, tot_ref, sums_out, tot_out, sem):
    copies = [
        pltpu.make_async_copy(sums_ref.at[pl.ds(0, rows)], sums_out, sem.at[0]),
        pltpu.make_async_copy(tot_ref, tot_out, sem.at[1]),
    ]
    for copy in copies:
        copy.start()
    for copy in copies:
        copy.wait()


def dense_on_device(images, references, candidates, inv_noise):
    rows_dev, pixels = images.shape
    n_cls, n_dp = lax.axis_size("cls"), lax.axis_size("dp")
    rot_count = references.shape[1]
    half = rot_count // n_dp
    pad = (half + 7) // 8 * 8
    side = math.isqrt(pixels)
    band = (3 * pad + 15) // 16 * 16
    plane_rows = 2 * SQUARE * rows_dev
    tiles = pixels // LANES
    width = pixels + LANES
    dma = pltpu.SemaphoreType.DMA
    vmem = pl.BlockSpec(memory_space=pltpu.VMEM)
    hbm = pl.BlockSpec(memory_space=pl.ANY)
    sums, totals = pl.pallas_call(
        functools.partial(dense_kernel, rows_dev, pixels, half, pad, side, n_cls),
        out_shape=(
            pltpu.VMEM((pad * tiles, LANES), jnp.float32),
            pltpu.VMEM((1, half), jnp.float32),
        ),
        in_specs=[hbm, vmem, vmem, vmem],
        out_specs=(vmem, vmem),
        scratch_shapes=[
            pltpu.VMEM((n_cls * n_dp, rows_dev, width), jnp.bfloat16),
            pltpu.VMEM((3 * band, pixels), jnp.bfloat16),
            pltpu.VMEM((2, PLANES, plane_rows, pixels), jnp.bfloat16),
            pltpu.VMEM((band, LANES), jnp.float32),
            pltpu.VMEM((3 * band, plane_rows), jnp.float32),
            pltpu.VMEM((PLANES, 3, band, plane_rows), jnp.float32),
            pltpu.VMEM((PLANES, 2, plane_rows), jnp.float32),
            pltpu.VMEM((2, band, 6 * plane_rows), jnp.bfloat16),
            pltpu.VMEM((band, pixels), jnp.float32),
            pltpu.VMEM((2, 2, 2 * plane_rows), jnp.float32),
            pltpu.VMEM((2, n_cls * n_dp, 2, 2 * plane_rows), jnp.float32),
            dma,
            dma((PLANES, 2, 4)),
            dma((2, n_cls)),
            dma((PLANES,)),
            dma((PLANES,)),
            dma((n_cls,)),
            dma((n_cls,)),
            dma((4 * PLANES,)),
            dma((n_cls,)),
            dma((2,)),
            dma((2,)),
        ],
        compiler_params=pltpu.CompilerParams(
            collective_id=0, has_side_effects=True, vmem_limit_bytes=56 << 20
        ),
    )(images, candidates.T, inv_noise.reshape(1, rows_dev), references)
    sums, totals = pl.pallas_call(
        functools.partial(deliver, half * tiles),
        out_shape=(
            jax.ShapeDtypeStruct((half * tiles, LANES), jnp.float32),
            jax.ShapeDtypeStruct((1, half), jnp.float32),
        ),
        in_specs=[vmem, vmem],
        out_specs=(hbm, hbm),
        scratch_shapes=[dma((2,))],
    )(*(pltpu.with_memory_space_constraint(v, pltpu.VMEM) for v in (sums, totals)))
    return sums.reshape(1, half, pixels), totals


def solution(mesh):
    placed = (
        P(("cls", "dp"), None),
        P("cls", None, None),
        P(("cls", "dp"), None),
        P(("cls", "dp")),
    )
    n_cls, n_dp = mesh.shape["cls"], mesh.shape["dp"]
    dense = n_cls == PLANES * SQUARE and n_dp == 2
    return jax.shard_map(
        dense_on_device if dense else on_device,
        mesh=mesh,
        in_specs=placed,
        out_specs=(P("cls", "dp", None), P("cls", "dp")),
        check_vma=False,
    )
```

```python
import functools
import math

import jax
import jax.numpy as jnp
from jax import lax
from jax.experimental import pallas as pl
from jax.experimental.pallas import tpu as pltpu
from jax.sharding import PartitionSpec as P

MESH = pl.DeviceIdType.MESH
LANES = 128
LOW = -1e30

OFFSETS = ((0, 0), (1, 0), (-1, 0), (0, 1), (0, -1), (1, 1), (1, -1), (-1, 1), (-1, -1))


def roll_flat(rows, shift_row, shift_col, side_len):
    result = jnp.roll(rows, shift_row * side_len, axis=1)
    if shift_col != 0:
        column = jnp.arange(side_len * side_len, dtype=jnp.int32) % side_len
        edge = 0 if shift_col > 0 else side_len - 1
        wrapped = jnp.roll(result, shift_col - shift_col * side_len, axis=1)
        plain = jnp.roll(result, shift_col, axis=1)
        result = jnp.where((column == edge)[None, :], wrapped, plain)
    return result


def shift_stack(rotated, side_len):
    return jnp.concatenate(
        [roll_flat(rotated, shift_row, shift_col, side_len) for shift_row, shift_col in OFFSETS],
        axis=0,
    )


def unshift_sum(summed_back, rot_count, side_len):
    square = summed_back.reshape(len(OFFSETS), rot_count, side_len * side_len)
    result = jnp.zeros((rot_count, side_len * side_len), jnp.float32)
    for position, offset in enumerate(OFFSETS):
        result = result + roll_flat(square[position], -offset[0], -offset[1], side_len)
    return result


def on_device(images, references, candidates, inv_noise):
    rows_dev, top_count = candidates.shape
    cls_dev, rot_count, pixels = references.shape
    side_len = math.isqrt(pixels)
    shift_count = len(OFFSETS)
    orient_count = rot_count * shift_count
    n_cls = lax.axis_size("cls")
    classes = cls_dev * n_cls
    slot_depth = max(2, (3 * rows_dev * top_count + 2 * classes - 1) // (2 * classes))
    owner_slots = cls_dev * slot_depth
    slots_all = n_cls * owner_slots
    member = jnp.sum(
        (candidates[:, :, None] == jnp.arange(classes, dtype=jnp.int32)[None, None, :]).astype(
            jnp.int32
        ),
        axis=1,
    )
    earlier = jnp.arange(rows_dev)[:, None] > jnp.arange(rows_dev)[None, :]
    before = jnp.sum(earlier.astype(jnp.int32)[:, :, None] * member[None, :, :], axis=1)
    slot_rank = jnp.take_along_axis(before, candidates, axis=1)
    slot_index = candidates // cls_dev * owner_slots + candidates % cls_dev * slot_depth + slot_rank
    flat_slot = slot_index.reshape(-1)
    source = (
        jnp.full((slots_all,), rows_dev, jnp.int32)
        .at[flat_slot]
        .set(jnp.repeat(jnp.arange(rows_dev, dtype=jnp.int32), top_count))
    )
    images_pad = jnp.concatenate([images, jnp.zeros((1, pixels), jnp.bfloat16)], axis=0)
    noise_pad = jnp.concatenate([inv_noise, jnp.zeros((1,), jnp.bfloat16)], axis=0)
    send_img = images_pad[source].reshape(n_cls, owner_slots * pixels)
    send_noise = noise_pad[source].reshape(n_cls, owner_slots)
    recv_img, recv_noise = (
        lax.all_to_all(send_img, "cls", split_axis=0, concat_axis=0, tiled=True),
        lax.all_to_all(send_noise, "cls", split_axis=0, concat_axis=0, tiled=True),
    )
    live_list = []
    class_pos = 0
    rows_img = recv_img.reshape(n_cls * slot_depth, pixels)
    rows_noise = recv_noise.reshape(-1).astype(jnp.float32)
    shifted = shift_stack(references[class_pos], side_len)
    ref_norms = jnp.sum(jnp.square(references[class_pos].astype(jnp.float32)), axis=1)
    products = lax.dot_general(
        rows_img, shifted, (((1,), (1,)), ((), ())), preferred_element_type=jnp.float32
    )
    class_scores = rows_noise[:, None] * (
        products - 0.5 * jnp.tile(ref_norms, shift_count)[None, :]
    )
    rows_list = [rows_img]
    live_list.append(rows_noise > 0)
    score_list = [class_scores]
    send_scores = jnp.concatenate(
        [part_scores.reshape(n_cls, slot_depth * orient_count) for part_scores in score_list],
        axis=1,
    )
    home_scores = lax.all_to_all(send_scores, "cls", split_axis=0, concat_axis=0, tiled=True)
    own_scores = home_scores.reshape(slots_all, orient_count)[slot_index]
    row_peak = jnp.max(own_scores, axis=(1, 2))
    norm_total = jnp.sum(jnp.exp(own_scores - row_peak[:, None, None]), axis=(1, 2))
    home_weights = (
        jnp.exp(own_scores - row_peak[:, None, None]) / norm_total[:, None, None]
    ).astype(jnp.bfloat16)
    slot_weights = (
        jnp.zeros((slots_all, orient_count), jnp.bfloat16)
        .at[flat_slot]
        .set(home_weights.reshape(-1, orient_count))
    )
    weights = lax.all_to_all(
        slot_weights.reshape(n_cls, owner_slots * orient_count),
        "cls",
        split_axis=0,
        concat_axis=0,
        tiled=True,
    )
    weight_rows = [weights.reshape(n_cls * slot_depth, orient_count)]
    class_pos = 0
    row_weights = weight_rows[class_pos]
    summed_back = lax.dot_general(
        row_weights,
        rows_list[class_pos],
        (((0,), (0,)), ((), ())),
        preferred_element_type=jnp.float32,
    )
    sums_list = [unshift_sum(summed_back, rot_count, side_len)]
    weight_list = [
        jnp.sum(row_weights.astype(jnp.float32), axis=0).reshape(shift_count, rot_count).sum(axis=0)
    ]
    local_sums = jnp.stack(sums_list, axis=0)
    local_weights = jnp.stack(weight_list, axis=0)
    class_sums, class_weights = (
        lax.psum_scatter(local_sums, "dp", scatter_dimension=1, tiled=True),
        lax.psum_scatter(local_weights, "dp", scatter_dimension=1, tiled=True),
    )
    return (class_sums, class_weights)


PLANES = 4
SQUARE = 4
BIG = 1e30
PIECES = 4
END = (
    4, 16, 32, 5, 17, 33, 6, 18, 34, 7, 19, 35, 20, 36, 8, 37, 48, 9, 21, 38,
    10, 49, 50, 11, 22, 39, 12, 23, 51, 13, 40, 52, 14, 24, 41, 15, 42, 53, 25, 43,
    26, 54, 27, 44, 28, 55, 29, 45, 46, 56, 30, 47, 57, 58, 31, 59, 60, 61, 62, 63,
)
MID = (
    4, 8, 16, 32, 5, 9, 17, 33, 6, 10, 18, 34, 7, 11, 19, 35, 12, 20, 36, 13,
    24, 40, 14, 37, 48, 15, 21, 41, 25, 38, 42, 49, 22, 50, 26, 39, 23, 43, 27, 51,
    28, 44, 45, 52, 29, 46, 47, 56, 30, 54, 53, 58, 31, 55, 57, 59, 60, 62, 61, 63,
)


def dense_kernel(
    rows_dev, pixels, half, pad, side, n_cls,
    img_ref, cand_ref, noise_ref, ref_ref, sums_ref, tot_ref,
    held, shifted, offset, acc, expo, peaks, wts, back, mine, stats,
    own_sem, send_sem, recv_sem, part_send, part_recv,
    st_send, st_recv,
):
    cls = lax.axis_index("cls")
    d = lax.axis_index("dp")
    z, y, x = cls // 4, (cls // 2) % 2, cls % 2
    other = 1 - d
    me = cls * 2 + d
    n_dev = n_cls * 2
    width = held.shape[2]
    lots = width // LANES
    edges = [q * lots // PIECES * LANES for q in range(PIECES + 1)]
    band = shifted.shape[0] // 3
    tiles = pixels // LANES
    plane_rows = 2 * SQUARE * rows_dev

    def block(bz, by, bx):
        return bz * 4 + by * 2 + bx

    t = z // 2
    order = [z, z + 1 - 2 * (z % 2), 2 - t, 3 - 3 * t]
    x_dev = {"cls": block(z, y, 1 - x), "dp": d}
    y_dev = {"cls": block(z, 1 - y, x), "dp": d}
    in_dev = {"cls": block(1 + z % 2, y, x), "dp": d}
    out_dev = {"cls": block(3 * (z // 2), y, x), "dp": d}
    middle = jnp.logical_or(z == 1, z == 2)
    border = jnp.logical_not(middle)
    core_dev = {"cls": cls, "dp": other}

    barrier = pltpu.get_barrier_semaphore()

    def greet(dev):
        pl.semaphore_signal(barrier, inc=1, device_id=dev, device_id_type=MESH)

    for dev in (x_dev, y_dev, core_dev, in_dev):
        greet(dev)
    pl.when(middle)(lambda: greet(out_dev))

    def slot(b, core=d):
        return (b // SQUARE) * 2 * SQUARE + core * SQUARE + b % SQUARE

    local = pltpu.make_async_copy(img_ref, held.at[slot(cls), :, pl.ds(0, pixels)], own_sem)
    local.start()

    def describe():
        eye = (
            lax.broadcasted_iota(jnp.int32, (rows_dev, rows_dev), 0)
            == lax.broadcasted_iota(jnp.int32, (rows_dev, rows_dev), 1)
        ).astype(jnp.float32).astype(jnp.bfloat16)
        dims = (((1,), (1,)), ((), ()))
        names = lax.dot_general(
            eye, cand_ref[...].astype(jnp.float32).astype(jnp.bfloat16), dims, preferred_element_type=jnp.float32
        )
        noise = jnp.broadcast_to(noise_ref[...].astype(jnp.float32), (8, rows_dev)).astype(jnp.bfloat16)
        level = lax.dot_general(eye, noise, dims, preferred_element_type=jnp.float32)[:, 0:1]
        lanes = lax.broadcasted_iota(jnp.int32, (rows_dev, LANES), 1).astype(jnp.float32)
        named = names[:, 0:1] == lanes
        for k in range(1, cand_ref.shape[0]):
            named = jnp.logical_or(named, names[:, k:k + 1] == lanes)
        held[slot(cls), :, pixels:pixels + LANES] = jnp.where(named, level, 0.0).astype(jnp.bfloat16)

    describe()
    local.wait()

    def moves(first, second):
        row = lax.broadcasted_iota(jnp.int32, (LANES, 2 * LANES), 0)
        col = lax.broadcasted_iota(jnp.int32, (LANES, 2 * LANES), 1)
        step = jnp.where(col < LANES, first, second)
        source = jnp.bitwise_or(jnp.bitwise_and(col, side), jnp.bitwise_and(col + step, side - 1))
        return (row == source).astype(jnp.float32).astype(jnp.bfloat16)

    def left(v):
        return jnp.concatenate([v[:, LANES:], v[:, :LANES]], axis=1)

    def build():
        row = lax.broadcasted_iota(jnp.int32, (pad, 2 * half), 0)
        col = lax.broadcasted_iota(jnp.int32, (pad, 2 * half), 1)
        pick = jnp.logical_and(col == row + d * half, row < half).astype(jnp.float32).astype(jnp.bfloat16)
        width_c = pixels // 8
        for c in range(8):
            cols = pl.ds(c * width_c, width_c)
            back[0:pad, cols] = jnp.dot(pick, ref_ref[0, :, cols], preferred_element_type=jnp.float32)
        for i in range(pad // 8):
            v = back[8 * i:8 * i + 8, :]
            back[pad + 8 * i:pad + 8 * i + 8, :] = pltpu.roll(v, side, 1)
            back[2 * pad + 8 * i:2 * pad + 8 * i + 8, :] = pltpu.roll(v, pixels - side, 1)
        if band > 3 * pad:
            back[3 * pad:band, :] = jnp.zeros((band - 3 * pad, pixels), jnp.float32)
        energy = 0.5 * jnp.sum(jnp.square(back[0:pad, :]), axis=1, keepdims=True)
        spare = lax.broadcasted_iota(jnp.int32, (pad, 1), 0) >= half
        energy = jnp.where(spare, BIG, energy)
        for dy in range(3):
            offset[dy * pad:(dy + 1) * pad, :] = jnp.broadcast_to(energy, (pad, LANES))
        if band > 3 * pad:
            offset[3 * pad:band, :] = jnp.full((band - 3 * pad, LANES), BIG, jnp.float32)
        both = moves(-1, 1)
        for j in range(tiles):
            cols = pl.ds(j * LANES, LANES)
            base = back[0:band, cols].astype(jnp.bfloat16)
            pair = jnp.dot(base, both, preferred_element_type=jnp.float32).astype(jnp.bfloat16)
            shifted[0:band, cols] = base
            shifted[band:2 * band, cols] = pair[:, 0:LANES]
            shifted[2 * band:3 * band, cols] = pair[:, LANES:2 * LANES]

    build()
    pl.semaphore_wait(barrier, 4 + jnp.where(middle, 1, 0))

    def remote(src, dst, send, recv, dev):
        return pltpu.make_async_remote_copy(
            src_ref=src, dst_ref=dst, send_sem=send, recv_sem=recv, device_id=dev, device_id_type=MESH
        )

    def span(b, first, last, core=d):
        return held.at[slot(b, core), :, pl.ds(edges[first], edges[last] - edges[first])]

    sent = {True: [], False: []}

    def one_piece(index, code, dev):
        b, q = where_from(code), code % 4
        ref = span(b, q, q + 1)
        return remote(ref, ref, send_sem.at[index], recv_sem.at[q, b], dev)

    def pass_on(inner, code, dev):
        sent[inner].append(code)
        one_piece(len(sent[inner]) - 1, code, dev).start()

    def where_from(code):
        kind, k = code // 16, code // 4 % 4
        return block(order[k], (y, y, 1 - y, 1 - y)[kind], (x, 1 - x, x, 1 - x)[kind])

    def forward(inner, code):
        kind, k, q = code // 16, code // 4 % 4, code % 4
        low = q < PIECES // 2
        devs = []
        if kind == 0:
            if inner:
                devs = [out_dev, in_dev] if k == 0 else [in_dev if k == 1 else out_dev]
            elif k == 0:
                devs = [in_dev]
            devs = devs + [x_dev, y_dev]
        elif kind == 1 and not low:
            devs = [y_dev]
        elif kind == 2 and low:
            devs = [x_dev]
        for dev in devs:
            pass_on(inner, code, dev)

    def to_core(code):
        b, part = where_from(code), code % 4 // 2
        ref = span(b, 2 * part, 2 * part + 2)
        return remote(ref, ref, part_send.at[code // 4, part], part_recv.at[part, b], core_dev)

    def take(inner, code, done):
        one_piece(0, code, x_dev).wait_recv()
        forward(inner, code)
        if code ^ 1 in done:
            to_core(code).start()

    def wait_core(b):
        for part in range(2):
            ref = span(b, 2 * part, 2 * part + 2, other)
            remote(ref, ref, part_send.at[0, 0], part_recv.at[part, b], core_dev).wait_recv()

    depth = pixels // 4

    def chunk_cols(c):
        return pl.ds(pl.multiple_of(c * depth, depth), depth)

    one = (lax.broadcasted_iota(jnp.int32, (8, LANES), 1) == cls).astype(jnp.float32).astype(jnp.bfloat16)

    def multiply(plane, c):
        first = plane * 2 * SQUARE
        cols = pl.ds(c * depth, depth)
        right = held[pl.ds(first, 2 * SQUARE), :, cols].reshape(plane_rows, depth)
        value = lax.dot_general(
            shifted[:, cols], right, (((1,), (1,)), ((), ())), preferred_element_type=jnp.float32
        )
        acc[...] = value if c == 0 else acc[...] + value

    def score(plane):
        prod = acc[...]
        first = plane * 2 * SQUARE
        meta = held[pl.ds(first, 2 * SQUARE), :, pixels:pixels + LANES].reshape(plane_rows, LANES)
        noise = lax.dot_general(one, meta, (((1,), (1,)), ((), ())), preferred_element_type=jnp.float32)[0:1, :]
        live = noise > 0
        value = noise[None] * (prod.reshape(3, band, plane_rows) - offset[...][None])
        peak = jnp.max(jnp.max(value, axis=0), axis=0, keepdims=True)
        peak = jnp.where(live, peak, LOW)
        grown = jnp.where(live[None], jnp.exp(value - peak[None]), 0.0)
        total = jnp.sum(jnp.sum(grown, axis=0), axis=0, keepdims=True)
        peaks[plane, 0:1, :] = peak
        peaks[plane, 1:2, :] = total
        expo[plane] = grown

    pairs = ((1, 2), (0, 3))

    def stat(m, j):
        t = (me + j) % n_dev
        return remote(mine.at[m], stats.at[m, me], st_send.at[m], st_recv.at[m], {"cls": t // 2, "dp": t % 2})

    def send_stats(m):
        for g, plane in enumerate(pairs[m]):
            mine[m, :, g * plane_rows:(g + 1) * plane_rows] = peaks[plane]
        stats[m, me] = mine[m]

        def send(j, carry):
            stat(m, j).start()
            return carry

        lax.fori_loop(1, n_dev, send, 0)

    def all_of(m, sem):
        ref = stats.at[m, pl.ds(0, n_dev - 1)]
        return pltpu.make_async_copy(ref, ref, sem.at[m])

    def weigh(m):
        all_of(m, st_recv).wait()
        every = stats[m]
        top = jnp.max(every[:, 0:1, :], axis=0)
        norm = jnp.sum(every[:, 1:2, :] * jnp.exp(every[:, 0:1, :] - top[None]), axis=0)
        factor = jnp.exp(mine[m, 0:1, :] - top) / norm
        flat = jnp.zeros((band, plane_rows), jnp.float32)
        for g, plane in enumerate(pairs[m]):
            weight = (expo[plane] * factor[None, :, g * plane_rows:(g + 1) * plane_rows]).astype(jnp.bfloat16)
            for dx in range(3):
                wts[m, dx * band:(dx + 1) * band, g * plane_rows:(g + 1) * plane_rows] = weight[dx]
            flat = flat + jnp.sum(weight.astype(jnp.float32), axis=0)
        return sum(flat[dy * pad:(dy + 1) * pad] for dy in range(3))

    def project(m):
        def part(c, carry):
            cols = pl.ds(c * depth, depth)
            right = jnp.concatenate(
                [
                    held[plane * 2 * SQUARE:(plane + 1) * 2 * SQUARE, :, cols].reshape(plane_rows, depth)
                    for plane in pairs[m]
                ],
                axis=0,
            )
            value = jnp.dot(wts[m], right, preferred_element_type=jnp.float32)
            back[:, cols] = value if m == 0 else back[:, cols] + value
            return carry

        for c in range(4):
            part(c, 0)

    def core_in(k):
        for by in (0, 1):
            for bx in (0, 1):
                wait_core(block(order[k], by, bx))

    def diagonal(k):
        b = block(order[k], 1 - y, 1 - x)
        piece(b, part_a, y_send.at[k], a_recv, x_dev).wait_recv()
        piece(b, part_b, x_send.at[k], b_recv, y_dev).wait_recv()
        go(to_core(3 * PLANES + k, b))

    work = []

    def queue_score(k):
        work.append(lambda: (core_in(k), multiply(order[k], 0), multiply(order[k], 1)))
        work.append(lambda: (multiply(order[k], 2), multiply(order[k], 3), score(order[k])))

    def idle():
        if work:
            work.pop(0)()

    def drain():
        while work:
            idle()

    def send_own(inner):
        for q in range(PIECES):
            forward(inner, q)

    pl.when(border)(lambda: send_own(False))
    pl.when(middle)(lambda: send_own(True))
    to_core(0).start()
    to_core(2).start()
    ready = {}
    for codes in (END, MID):
        for i, code in enumerate(codes):
            ready[code // 4 % 4] = max(ready.get(code // 4 % 4, 0), i)
    for i in range(len(END)):
        pl.when(border)(lambda: take(False, END[i], END[:i]))
        pl.when(middle)(lambda: take(True, MID[i], MID[:i]))
        for k in range(3):
            if i == ready[k] + 2:
                queue_score(k)
                if k == 2:
                    work.append(lambda: send_stats(0))
        if i % 1 == 0:
            idle()
    for k in range(3):
        if len(END) <= ready[k] + 2:
            queue_score(k)
            if k == 2:
                work.append(lambda: send_stats(0))
    drain()
    queue_score(3)
    drain()
    send_stats(1)

    def all_sent(inner):
        for index, code in enumerate(sent[inner]):
            one_piece(index, code, x_dev).wait_send()

    pl.when(border)(lambda: all_sent(False))
    pl.when(middle)(lambda: all_sent(True))
    for code in sorted(set(END + (0, 1, 2, 3))):
        if code % 2 == 0:
            to_core(code).wait_send()
    flat = weigh(0)
    project(0)
    flat = flat + weigh(1)
    project(1)

    both = moves(1, -1)

    def parts(v):
        high = v.astype(jnp.bfloat16)
        return high, (v - high.astype(jnp.float32)).astype(jnp.bfloat16)

    for i in range(pad // 8):
        lines = []
        for dx in range(3):
            same, above, below = (
                back[dx * band + k * pad + 8 * i:dx * band + k * pad + 8 * i + 8, :] for k in range(3)
            )
            lines.append(same + pltpu.roll(left(above) + below, side, 1))
        back[8 * i:8 * i + 8, :] = lines[0]
        back[band + 8 * i:band + 8 * i + 8, :] = lines[1]
        back[2 * band + 8 * i:2 * band + 8 * i + 8, :] = lines[2]
    span_count = 8
    for c in range(0, tiles, span_count):
        total = None
        for dx in (1, 2):
            chunks = [
                back[dx * band:dx * band + pad, (c + u) * LANES:(c + u + 1) * LANES] for u in range(span_count)
            ]
            source = jnp.concatenate(chunks, axis=0)
            move = both[:, (dx - 1) * LANES:dx * LANES]
            value = jnp.dot(
                jnp.concatenate(parts(source), axis=1),
                jnp.concatenate([move, move], axis=0),
                preferred_element_type=jnp.float32,
            )
            total = value if total is None else total + value
        for u in range(span_count):
            value = total[u * pad:(u + 1) * pad] + back[0:pad, (c + u) * LANES:(c + u + 1) * LANES]
            for i in range(pad // 8):
                sums_ref[pl.ds(8 * i * tiles + c + u, 8, stride=tiles), :] = value[8 * i:8 * i + 8]
    column = jnp.sum(flat, axis=1, keepdims=True)
    eye = lax.broadcasted_iota(jnp.int32, (pad, LANES), 0) == lax.broadcasted_iota(jnp.int32, (pad, LANES), 1)
    tot_ref[...] = jnp.sum(jnp.where(eye, column, 0.0), axis=0, keepdims=True)[:, 0:half]
    for m in range(2):
        all_of(m, st_send).wait()


def deliver(rows, sums_ref, tot_ref, sums_out, tot_out, sem):
    copies = [
        pltpu.make_async_copy(sums_ref.at[pl.ds(0, rows)], sums_out, sem.at[0]),
        pltpu.make_async_copy(tot_ref, tot_out, sem.at[1]),
    ]
    for copy in copies:
        copy.start()
    for copy in copies:
        copy.wait()


def dense_on_device(images, references, candidates, inv_noise):
    rows_dev, pixels = images.shape
    n_cls, n_dp = lax.axis_size("cls"), lax.axis_size("dp")
    rot_count = references.shape[1]
    half = rot_count // n_dp
    pad = (half + 7) // 8 * 8
    side = math.isqrt(pixels)
    band = (3 * pad + 15) // 16 * 16
    plane_rows = 2 * SQUARE * rows_dev
    tiles = pixels // LANES
    width = pixels + LANES
    dma = pltpu.SemaphoreType.DMA
    vmem = pl.BlockSpec(memory_space=pltpu.VMEM)
    hbm = pl.BlockSpec(memory_space=pl.ANY)
    sums, totals = pl.pallas_call(
        functools.partial(dense_kernel, rows_dev, pixels, half, pad, side, n_cls),
        out_shape=(
            pltpu.VMEM((pad * tiles, LANES), jnp.float32),
            pltpu.VMEM((1, half), jnp.float32),
        ),
        in_specs=[hbm, vmem, vmem, vmem],
        out_specs=(vmem, vmem),
        scratch_shapes=[
            pltpu.VMEM((n_cls * n_dp, rows_dev, width), jnp.bfloat16),
            pltpu.VMEM((3 * band, pixels), jnp.bfloat16),
            pltpu.VMEM((band, LANES), jnp.float32),
            pltpu.VMEM((3 * band, plane_rows), jnp.float32),
            pltpu.VMEM((PLANES, 3, band, plane_rows), jnp.float32),
            pltpu.VMEM((PLANES, 2, plane_rows), jnp.float32),
            pltpu.VMEM((2, 3 * band, 2 * plane_rows), jnp.bfloat16),
            pltpu.VMEM((3 * band, pixels), jnp.float32),
            pltpu.VMEM((2, 2, 2 * plane_rows), jnp.float32),
            pltpu.VMEM((2, n_cls * n_dp, 2, 2 * plane_rows), jnp.float32),
            dma,
            dma((96,)),
            dma((PIECES, n_cls)),
            dma((4 * PLANES, 2)),
            dma((2, n_cls)),
            dma((2,)),
            dma((2,)),
        ],
        compiler_params=pltpu.CompilerParams(
            collective_id=0, has_side_effects=True, vmem_limit_bytes=56 << 20
        ),
    )(images, candidates.T, inv_noise.reshape(1, rows_dev), references)
    sums, totals = pl.pallas_call(
        functools.partial(deliver, half * tiles),
        out_shape=(
            jax.ShapeDtypeStruct((half * tiles, LANES), jnp.float32),
            jax.ShapeDtypeStruct((1, half), jnp.float32),
        ),
        in_specs=[vmem, vmem],
        out_specs=(hbm, hbm),
        scratch_shapes=[dma((2,))],
    )(*(pltpu.with_memory_space_constraint(v, pltpu.VMEM) for v in (sums, totals)))
    return sums.reshape(1, half, pixels), totals


def solution(mesh):
    placed = (
        P(("cls", "dp"), None),
        P("cls", None, None),
        P(("cls", "dp"), None),
        P(("cls", "dp")),
    )
    n_cls, n_dp = mesh.shape["cls"], mesh.shape["dp"]
    dense = n_cls == PLANES * SQUARE and n_dp == 2
    return jax.shard_map(
        dense_on_device if dense else on_device,
        mesh=mesh,
        in_specs=placed,
        out_specs=(P("cls", "dp", None), P("cls", "dp")),
        check_vma=False,
    )
```

```python
import functools
import math

import jax
import jax.numpy as jnp
from jax import lax
from jax.experimental import pallas as pl
from jax.experimental.pallas import tpu as pltpu
from jax.sharding import PartitionSpec as P

MESH = pl.DeviceIdType.MESH
LANES = 128
LOW = -1e30

OFFSETS = ((0, 0), (1, 0), (-1, 0), (0, 1), (0, -1), (1, 1), (1, -1), (-1, 1), (-1, -1))


def roll_flat(rows, shift_row, shift_col, side_len):
    result = jnp.roll(rows, shift_row * side_len, axis=1)
    if shift_col != 0:
        column = jnp.arange(side_len * side_len, dtype=jnp.int32) % side_len
        edge = 0 if shift_col > 0 else side_len - 1
        wrapped = jnp.roll(result, shift_col - shift_col * side_len, axis=1)
        plain = jnp.roll(result, shift_col, axis=1)
        result = jnp.where((column == edge)[None, :], wrapped, plain)
    return result


def shift_stack(rotated, side_len):
    return jnp.concatenate(
        [roll_flat(rotated, shift_row, shift_col, side_len) for shift_row, shift_col in OFFSETS],
        axis=0,
    )


def unshift_sum(summed_back, rot_count, side_len):
    square = summed_back.reshape(len(OFFSETS), rot_count, side_len * side_len)
    result = jnp.zeros((rot_count, side_len * side_len), jnp.float32)
    for position, offset in enumerate(OFFSETS):
        result = result + roll_flat(square[position], -offset[0], -offset[1], side_len)
    return result


def on_device(images, references, candidates, inv_noise):
    rows_dev, top_count = candidates.shape
    cls_dev, rot_count, pixels = references.shape
    side_len = math.isqrt(pixels)
    shift_count = len(OFFSETS)
    orient_count = rot_count * shift_count
    n_cls = lax.axis_size("cls")
    classes = cls_dev * n_cls
    slot_depth = max(2, (3 * rows_dev * top_count + 2 * classes - 1) // (2 * classes))
    owner_slots = cls_dev * slot_depth
    slots_all = n_cls * owner_slots
    member = jnp.sum(
        (candidates[:, :, None] == jnp.arange(classes, dtype=jnp.int32)[None, None, :]).astype(
            jnp.int32
        ),
        axis=1,
    )
    earlier = jnp.arange(rows_dev)[:, None] > jnp.arange(rows_dev)[None, :]
    before = jnp.sum(earlier.astype(jnp.int32)[:, :, None] * member[None, :, :], axis=1)
    slot_rank = jnp.take_along_axis(before, candidates, axis=1)
    slot_index = candidates // cls_dev * owner_slots + candidates % cls_dev * slot_depth + slot_rank
    flat_slot = slot_index.reshape(-1)
    source = (
        jnp.full((slots_all,), rows_dev, jnp.int32)
        .at[flat_slot]
        .set(jnp.repeat(jnp.arange(rows_dev, dtype=jnp.int32), top_count))
    )
    images_pad = jnp.concatenate([images, jnp.zeros((1, pixels), jnp.bfloat16)], axis=0)
    noise_pad = jnp.concatenate([inv_noise, jnp.zeros((1,), jnp.bfloat16)], axis=0)
    send_img = images_pad[source].reshape(n_cls, owner_slots * pixels)
    send_noise = noise_pad[source].reshape(n_cls, owner_slots)
    recv_img, recv_noise = (
        lax.all_to_all(send_img, "cls", split_axis=0, concat_axis=0, tiled=True),
        lax.all_to_all(send_noise, "cls", split_axis=0, concat_axis=0, tiled=True),
    )
    live_list = []
    class_pos = 0
    rows_img = recv_img.reshape(n_cls * slot_depth, pixels)
    rows_noise = recv_noise.reshape(-1).astype(jnp.float32)
    shifted = shift_stack(references[class_pos], side_len)
    ref_norms = jnp.sum(jnp.square(references[class_pos].astype(jnp.float32)), axis=1)
    products = lax.dot_general(
        rows_img, shifted, (((1,), (1,)), ((), ())), preferred_element_type=jnp.float32
    )
    class_scores = rows_noise[:, None] * (
        products - 0.5 * jnp.tile(ref_norms, shift_count)[None, :]
    )
    rows_list = [rows_img]
    live_list.append(rows_noise > 0)
    score_list = [class_scores]
    send_scores = jnp.concatenate(
        [part_scores.reshape(n_cls, slot_depth * orient_count) for part_scores in score_list],
        axis=1,
    )
    home_scores = lax.all_to_all(send_scores, "cls", split_axis=0, concat_axis=0, tiled=True)
    own_scores = home_scores.reshape(slots_all, orient_count)[slot_index]
    row_peak = jnp.max(own_scores, axis=(1, 2))
    norm_total = jnp.sum(jnp.exp(own_scores - row_peak[:, None, None]), axis=(1, 2))
    home_weights = (
        jnp.exp(own_scores - row_peak[:, None, None]) / norm_total[:, None, None]
    ).astype(jnp.bfloat16)
    slot_weights = (
        jnp.zeros((slots_all, orient_count), jnp.bfloat16)
        .at[flat_slot]
        .set(home_weights.reshape(-1, orient_count))
    )
    weights = lax.all_to_all(
        slot_weights.reshape(n_cls, owner_slots * orient_count),
        "cls",
        split_axis=0,
        concat_axis=0,
        tiled=True,
    )
    weight_rows = [weights.reshape(n_cls * slot_depth, orient_count)]
    class_pos = 0
    row_weights = weight_rows[class_pos]
    summed_back = lax.dot_general(
        row_weights,
        rows_list[class_pos],
        (((0,), (0,)), ((), ())),
        preferred_element_type=jnp.float32,
    )
    sums_list = [unshift_sum(summed_back, rot_count, side_len)]
    weight_list = [
        jnp.sum(row_weights.astype(jnp.float32), axis=0).reshape(shift_count, rot_count).sum(axis=0)
    ]
    local_sums = jnp.stack(sums_list, axis=0)
    local_weights = jnp.stack(weight_list, axis=0)
    class_sums, class_weights = (
        lax.psum_scatter(local_sums, "dp", scatter_dimension=1, tiled=True),
        lax.psum_scatter(local_weights, "dp", scatter_dimension=1, tiled=True),
    )
    return (class_sums, class_weights)


PLANES = 4
SQUARE = 4
BIG = 1e30
PIECES = 4
END = (
    4, 16, 32, 5, 17, 33, 6, 18, 34, 7, 19, 35, 20, 36, 8, 37, 48, 9, 21, 38,
    10, 49, 50, 11, 22, 39, 12, 23, 51, 13, 40, 52, 14, 24, 41, 15, 42, 53, 25, 43,
    26, 54, 27, 44, 28, 55, 29, 45, 46, 56, 30, 47, 57, 58, 31, 59, 60, 61, 62, 63,
)
MID = (
    4, 8, 16, 32, 5, 9, 17, 33, 6, 10, 18, 34, 7, 11, 19, 35, 12, 20, 36, 13,
    24, 40, 14, 37, 48, 15, 21, 41, 25, 38, 42, 49, 22, 50, 26, 39, 23, 43, 27, 51,
    28, 44, 45, 52, 29, 46, 47, 56, 30, 54, 53, 58, 31, 55, 57, 59, 60, 62, 61, 63,
)


def dense_kernel(
    rows_dev, pixels, half, pad, side, n_cls,
    img_ref, cand_ref, noise_ref, ref_ref, sums_ref, tot_ref,
    held, shifted, offset, acc, expo, peaks, wts, back, mine, stats,
    own_sem, send_sem, recv_sem, part_send, part_recv,
    st_send, st_recv,
):
    cls = lax.axis_index("cls")
    d = lax.axis_index("dp")
    z, y, x = cls // 4, (cls // 2) % 2, cls % 2
    other = 1 - d
    me = cls * 2 + d
    n_dev = n_cls * 2
    width = held.shape[2]
    lots = width // LANES
    edges = [q * lots // PIECES * LANES for q in range(PIECES + 1)]
    band = shifted.shape[0] // 3
    tiles = pixels // LANES
    plane_rows = 2 * SQUARE * rows_dev

    def block(bz, by, bx):
        return bz * 4 + by * 2 + bx

    t = z // 2
    order = [z, z + 1 - 2 * (z % 2), 2 - t, 3 - 3 * t]
    x_dev = {"cls": block(z, y, 1 - x), "dp": d}
    y_dev = {"cls": block(z, 1 - y, x), "dp": d}
    in_dev = {"cls": block(1 + z % 2, y, x), "dp": d}
    out_dev = {"cls": block(3 * (z // 2), y, x), "dp": d}
    middle = jnp.logical_or(z == 1, z == 2)
    border = jnp.logical_not(middle)
    core_dev = {"cls": cls, "dp": other}

    barrier = pltpu.get_barrier_semaphore()

    def greet(dev):
        pl.semaphore_signal(barrier, inc=1, device_id=dev, device_id_type=MESH)

    for dev in (x_dev, y_dev, core_dev, in_dev):
        greet(dev)
    pl.when(middle)(lambda: greet(out_dev))

    def slot(b, core=d):
        return (b // SQUARE) * 2 * SQUARE + core * SQUARE + b % SQUARE

    local = pltpu.make_async_copy(img_ref, held.at[slot(cls), :, pl.ds(0, pixels)], own_sem)
    local.start()

    def describe():
        eye = (
            lax.broadcasted_iota(jnp.int32, (rows_dev, rows_dev), 0)
            == lax.broadcasted_iota(jnp.int32, (rows_dev, rows_dev), 1)
        ).astype(jnp.float32).astype(jnp.bfloat16)
        dims = (((1,), (1,)), ((), ()))
        names = lax.dot_general(
            eye, cand_ref[...].astype(jnp.float32).astype(jnp.bfloat16), dims, preferred_element_type=jnp.float32
        )
        noise = jnp.broadcast_to(noise_ref[...].astype(jnp.float32), (8, rows_dev)).astype(jnp.bfloat16)
        level = lax.dot_general(eye, noise, dims, preferred_element_type=jnp.float32)[:, 0:1]
        lanes = lax.broadcasted_iota(jnp.int32, (rows_dev, LANES), 1).astype(jnp.float32)
        named = names[:, 0:1] == lanes
        for k in range(1, cand_ref.shape[0]):
            named = jnp.logical_or(named, names[:, k:k + 1] == lanes)
        held[slot(cls), :, pixels:pixels + LANES] = jnp.where(named, level, 0.0).astype(jnp.bfloat16)

    describe()
    local.wait()

    def moves(first, second):
        row = lax.broadcasted_iota(jnp.int32, (LANES, 2 * LANES), 0)
        col = lax.broadcasted_iota(jnp.int32, (LANES, 2 * LANES), 1)
        step = jnp.where(col < LANES, first, second)
        source = jnp.bitwise_or(jnp.bitwise_and(col, side), jnp.bitwise_and(col + step, side - 1))
        return (row == source).astype(jnp.float32).astype(jnp.bfloat16)

    def left(v):
        return jnp.concatenate([v[:, LANES:], v[:, :LANES]], axis=1)

    def build():
        row = lax.broadcasted_iota(jnp.int32, (pad, 2 * half), 0)
        col = lax.broadcasted_iota(jnp.int32, (pad, 2 * half), 1)
        pick = jnp.logical_and(col == row + d * half, row < half).astype(jnp.float32).astype(jnp.bfloat16)
        width_c = pixels // 8
        for c in range(8):
            cols = pl.ds(c * width_c, width_c)
            back[0:pad, cols] = jnp.dot(pick, ref_ref[0, :, cols], preferred_element_type=jnp.float32)
        for i in range(pad // 8):
            v = back[8 * i:8 * i + 8, :]
            back[pad + 8 * i:pad + 8 * i + 8, :] = pltpu.roll(v, side, 1)
            back[2 * pad + 8 * i:2 * pad + 8 * i + 8, :] = pltpu.roll(v, pixels - side, 1)
        if band > 3 * pad:
            back[3 * pad:band, :] = jnp.zeros((band - 3 * pad, pixels), jnp.float32)
        energy = 0.5 * jnp.sum(jnp.square(back[0:pad, :]), axis=1, keepdims=True)
        spare = lax.broadcasted_iota(jnp.int32, (pad, 1), 0) >= half
        energy = jnp.where(spare, BIG, energy)
        for dy in range(3):
            offset[dy * pad:(dy + 1) * pad, :] = jnp.broadcast_to(energy, (pad, LANES))
        if band > 3 * pad:
            offset[3 * pad:band, :] = jnp.full((band - 3 * pad, LANES), BIG, jnp.float32)
        both = moves(-1, 1)
        for j in range(tiles):
            cols = pl.ds(j * LANES, LANES)
            base = back[0:band, cols].astype(jnp.bfloat16)
            pair = jnp.dot(base, both, preferred_element_type=jnp.float32).astype(jnp.bfloat16)
            shifted[0:band, cols] = base
            shifted[band:2 * band, cols] = pair[:, 0:LANES]
            shifted[2 * band:3 * band, cols] = pair[:, LANES:2 * LANES]

    build()
    pl.semaphore_wait(barrier, 4 + jnp.where(middle, 1, 0))

    def remote(src, dst, send, recv, dev):
        return pltpu.make_async_remote_copy(
            src_ref=src, dst_ref=dst, send_sem=send, recv_sem=recv, device_id=dev, device_id_type=MESH
        )

    def span(b, first, last, core=d):
        return held.at[slot(b, core), :, pl.ds(edges[first], edges[last] - edges[first])]

    sent = {True: [], False: []}

    def one_piece(index, code, dev):
        b, q = where_from(code), code % 4
        ref = span(b, q, q + 1)
        return remote(ref, ref, send_sem.at[index], recv_sem.at[q, b], dev)

    def pass_on(inner, code, dev):
        sent[inner].append(code)
        one_piece(len(sent[inner]) - 1, code, dev).start()

    def where_from(code):
        kind, k = code // 16, code // 4 % 4
        return block(order[k], (y, y, 1 - y, 1 - y)[kind], (x, 1 - x, x, 1 - x)[kind])

    def forward(inner, code):
        kind, k, q = code // 16, code // 4 % 4, code % 4
        low = q < PIECES // 2
        devs = []
        if kind == 0:
            if inner:
                devs = [out_dev, in_dev] if k == 0 else [in_dev if k == 1 else out_dev]
            elif k == 0:
                devs = [in_dev]
            devs = devs + [x_dev, y_dev]
        elif kind == 1 and not low:
            devs = [y_dev]
        elif kind == 2 and low:
            devs = [x_dev]
        for dev in devs:
            pass_on(inner, code, dev)

    def to_core(code):
        b, part = where_from(code), code % 4 // 2
        ref = span(b, 2 * part, 2 * part + 2)
        return remote(ref, ref, part_send.at[code // 4, part], part_recv.at[part, b], core_dev)

    def take(inner, code, done):
        one_piece(0, code, x_dev).wait_recv()
        forward(inner, code)
        if code ^ 1 in done:
            to_core(code).start()

    def wait_core(b):
        for part in range(2):
            ref = span(b, 2 * part, 2 * part + 2, other)
            remote(ref, ref, part_send.at[0, 0], part_recv.at[part, b], core_dev).wait_recv()

    depth = pixels // 4

    def chunk_cols(c):
        return pl.ds(pl.multiple_of(c * depth, depth), depth)

    one = (lax.broadcasted_iota(jnp.int32, (8, LANES), 1) == cls).astype(jnp.float32).astype(jnp.bfloat16)

    def multiply(plane, c):
        first = plane * 2 * SQUARE
        cols = pl.ds(c * depth, depth)
        right = held[pl.ds(first, 2 * SQUARE), :, cols].reshape(plane_rows, depth)
        value = lax.dot_general(
            shifted[:, cols], right, (((1,), (1,)), ((), ())), preferred_element_type=jnp.float32
        )
        acc[...] = value if c == 0 else acc[...] + value

    def score(plane):
        prod = acc[...]
        first = plane * 2 * SQUARE
        meta = held[pl.ds(first, 2 * SQUARE), :, pixels:pixels + LANES].reshape(plane_rows, LANES)
        noise = lax.dot_general(one, meta, (((1,), (1,)), ((), ())), preferred_element_type=jnp.float32)[0:1, :]
        live = noise > 0
        value = noise[None] * (prod.reshape(3, band, plane_rows) - offset[...][None])
        peak = jnp.max(jnp.max(value, axis=0), axis=0, keepdims=True)
        peak = jnp.where(live, peak, LOW)
        grown = jnp.where(live[None], jnp.exp(value - peak[None]), 0.0)
        total = jnp.sum(jnp.sum(grown, axis=0), axis=0, keepdims=True)
        peaks[plane, 0:1, :] = peak
        peaks[plane, 1:2, :] = total
        expo[plane] = grown

    pairs = ((1, 2), (0, 3))

    def stat(m, target, core):
        return remote(mine.at[m], stats.at[m, me], st_send.at[m], st_recv.at[m], {"cls": target, "dp": core})

    def send_stats(m):
        for g, plane in enumerate(pairs[m]):
            mine[m, :, g * plane_rows:(g + 1) * plane_rows] = peaks[plane]
        for step in range(n_cls):
            far = cls + step
            target = jnp.where(far >= n_cls, far - n_cls, far)
            if step > 0:
                stat(m, target, d).start()
            stat(m, target, other).start()
        stats[m, me] = mine[m]

    def all_of(m, sem):
        ref = stats.at[m, pl.ds(0, n_dev - 1)]
        return pltpu.make_async_copy(ref, ref, sem.at[m])

    def weigh(m):
        all_of(m, st_recv).wait()
        every = stats[m]
        top = jnp.max(every[:, 0:1, :], axis=0)
        norm = jnp.sum(every[:, 1:2, :] * jnp.exp(every[:, 0:1, :] - top[None]), axis=0)
        factor = jnp.exp(mine[m, 0:1, :] - top) / norm
        flat = jnp.zeros((band, plane_rows), jnp.float32)
        for g, plane in enumerate(pairs[m]):
            weight = (expo[plane] * factor[None, :, g * plane_rows:(g + 1) * plane_rows]).astype(jnp.bfloat16)
            for dx in range(3):
                wts[m, dx * band:(dx + 1) * band, g * plane_rows:(g + 1) * plane_rows] = weight[dx]
            flat = flat + jnp.sum(weight.astype(jnp.float32), axis=0)
        return sum(flat[dy * pad:(dy + 1) * pad] for dy in range(3))

    def project(m):
        def part(c, carry):
            cols = pl.ds(c * depth, depth)
            right = jnp.concatenate(
                [
                    held[plane * 2 * SQUARE:(plane + 1) * 2 * SQUARE, :, cols].reshape(plane_rows, depth)
                    for plane in pairs[m]
                ],
                axis=0,
            )
            value = jnp.dot(wts[m], right, preferred_element_type=jnp.float32)
            back[:, cols] = value if m == 0 else back[:, cols] + value
            return carry

        for c in range(4):
            part(c, 0)

    def core_in(k):
        for by in (0, 1):
            for bx in (0, 1):
                wait_core(block(order[k], by, bx))

    def diagonal(k):
        b = block(order[k], 1 - y, 1 - x)
        piece(b, part_a, y_send.at[k], a_recv, x_dev).wait_recv()
        piece(b, part_b, x_send.at[k], b_recv, y_dev).wait_recv()
        go(to_core(3 * PLANES + k, b))

    work = []

    def queue_score(k):
        work.append(lambda: (core_in(k), multiply(order[k], 0), multiply(order[k], 1)))
        work.append(lambda: (multiply(order[k], 2), multiply(order[k], 3), score(order[k])))

    def idle():
        if work:
            work.pop(0)()

    def drain():
        while work:
            idle()

    def send_own(inner):
        for q in range(PIECES):
            forward(inner, q)

    pl.when(border)(lambda: send_own(False))
    pl.when(middle)(lambda: send_own(True))
    to_core(0).start()
    to_core(2).start()
    ready = {}
    for codes in (END, MID):
        for i, code in enumerate(codes):
            ready[code // 4 % 4] = max(ready.get(code // 4 % 4, 0), i)
    for i in range(len(END)):
        pl.when(border)(lambda: take(False, END[i], END[:i]))
        pl.when(middle)(lambda: take(True, MID[i], MID[:i]))
        for k in range(3):
            if i == ready[k] + 2:
                queue_score(k)
                if k == 2:
                    work.append(lambda: send_stats(0))
        if i % 1 == 0:
            idle()
    for k in range(3):
        if len(END) <= ready[k] + 2:
            queue_score(k)
            if k == 2:
                work.append(lambda: send_stats(0))
    drain()
    queue_score(3)
    drain()
    send_stats(1)

    def all_sent(inner):
        for index, code in enumerate(sent[inner]):
            one_piece(index, code, x_dev).wait_send()

    pl.when(border)(lambda: all_sent(False))
    pl.when(middle)(lambda: all_sent(True))
    for code in sorted(set(END + (0, 1, 2, 3))):
        if code % 2 == 0:
            to_core(code).wait_send()
    flat = weigh(0)
    project(0)
    flat = flat + weigh(1)
    project(1)

    both = moves(1, -1)

    def parts(v):
        high = v.astype(jnp.bfloat16)
        return high, (v - high.astype(jnp.float32)).astype(jnp.bfloat16)

    for i in range(pad // 8):
        lines = []
        for dx in range(3):
            same, above, below = (
                back[dx * band + k * pad + 8 * i:dx * band + k * pad + 8 * i + 8, :] for k in range(3)
            )
            lines.append(same + pltpu.roll(left(above) + below, side, 1))
        back[8 * i:8 * i + 8, :] = lines[0]
        back[band + 8 * i:band + 8 * i + 8, :] = lines[1]
        back[2 * band + 8 * i:2 * band + 8 * i + 8, :] = lines[2]
    span_count = 8
    for c in range(0, tiles, span_count):
        total = None
        for dx in (1, 2):
            chunks = [
                back[dx * band:dx * band + pad, (c + u) * LANES:(c + u + 1) * LANES] for u in range(span_count)
            ]
            source = jnp.concatenate(chunks, axis=0)
            move = both[:, (dx - 1) * LANES:dx * LANES]
            value = jnp.dot(
                jnp.concatenate(parts(source), axis=1),
                jnp.concatenate([move, move], axis=0),
                preferred_element_type=jnp.float32,
            )
            total = value if total is None else total + value
        for u in range(span_count):
            value = total[u * pad:(u + 1) * pad] + back[0:pad, (c + u) * LANES:(c + u + 1) * LANES]
            for i in range(pad // 8):
                sums_ref[pl.ds(8 * i * tiles + c + u, 8, stride=tiles), :] = value[8 * i:8 * i + 8]
    column = jnp.sum(flat, axis=1, keepdims=True)
    eye = lax.broadcasted_iota(jnp.int32, (pad, LANES), 0) == lax.broadcasted_iota(jnp.int32, (pad, LANES), 1)
    tot_ref[...] = jnp.sum(jnp.where(eye, column, 0.0), axis=0, keepdims=True)[:, 0:half]
    for m in range(2):
        all_of(m, st_send).wait()


def deliver(rows, sums_ref, tot_ref, sums_out, tot_out, sem):
    copies = [
        pltpu.make_async_copy(sums_ref.at[pl.ds(0, rows)], sums_out, sem.at[0]),
        pltpu.make_async_copy(tot_ref, tot_out, sem.at[1]),
    ]
    for copy in copies:
        copy.start()
    for copy in copies:
        copy.wait()


def dense_on_device(images, references, candidates, inv_noise):
    rows_dev, pixels = images.shape
    n_cls, n_dp = lax.axis_size("cls"), lax.axis_size("dp")
    rot_count = references.shape[1]
    half = rot_count // n_dp
    pad = (half + 7) // 8 * 8
    side = math.isqrt(pixels)
    band = (3 * pad + 15) // 16 * 16
    plane_rows = 2 * SQUARE * rows_dev
    tiles = pixels // LANES
    width = pixels + LANES
    dma = pltpu.SemaphoreType.DMA
    vmem = pl.BlockSpec(memory_space=pltpu.VMEM)
    hbm = pl.BlockSpec(memory_space=pl.ANY)
    sums, totals = pl.pallas_call(
        functools.partial(dense_kernel, rows_dev, pixels, half, pad, side, n_cls),
        out_shape=(
            pltpu.VMEM((pad * tiles, LANES), jnp.float32),
            pltpu.VMEM((1, half), jnp.float32),
        ),
        in_specs=[hbm, vmem, vmem, vmem],
        out_specs=(vmem, vmem),
        scratch_shapes=[
            pltpu.VMEM((n_cls * n_dp, rows_dev, width), jnp.bfloat16),
            pltpu.VMEM((3 * band, pixels), jnp.bfloat16),
            pltpu.VMEM((band, LANES), jnp.float32),
            pltpu.VMEM((3 * band, plane_rows), jnp.float32),
            pltpu.VMEM((PLANES, 3, band, plane_rows), jnp.float32),
            pltpu.VMEM((PLANES, 2, plane_rows), jnp.float32),
            pltpu.VMEM((2, 3 * band, 2 * plane_rows), jnp.bfloat16),
            pltpu.VMEM((3 * band, pixels), jnp.float32),
            pltpu.VMEM((2, 2, 2 * plane_rows), jnp.float32),
            pltpu.VMEM((2, n_cls * n_dp, 2, 2 * plane_rows), jnp.float32),
            dma,
            dma((96,)),
            dma((PIECES, n_cls)),
            dma((4 * PLANES, 2)),
            dma((2, n_cls)),
            dma((2,)),
            dma((2,)),
        ],
        compiler_params=pltpu.CompilerParams(
            collective_id=0, has_side_effects=True, vmem_limit_bytes=56 << 20
        ),
    )(images, candidates.T, inv_noise.reshape(1, rows_dev), references)
    sums, totals = pl.pallas_call(
        functools.partial(deliver, half * tiles),
        out_shape=(
            jax.ShapeDtypeStruct((half * tiles, LANES), jnp.float32),
            jax.ShapeDtypeStruct((1, half), jnp.float32),
        ),
        in_specs=[vmem, vmem],
        out_specs=(hbm, hbm),
        scratch_shapes=[dma((2,))],
    )(*(pltpu.with_memory_space_constraint(v, pltpu.VMEM) for v in (sums, totals)))
    return sums.reshape(1, half, pixels), totals


def solution(mesh):
    placed = (
        P(("cls", "dp"), None),
        P("cls", None, None),
        P(("cls", "dp"), None),
        P(("cls", "dp")),
    )
    n_cls, n_dp = mesh.shape["cls"], mesh.shape["dp"]
    dense = n_cls == PLANES * SQUARE and n_dp == 2
    return jax.shard_map(
        dense_on_device if dense else on_device,
        mesh=mesh,
        in_specs=placed,
        out_specs=(P("cls", "dp", None), P("cls", "dp")),
        check_vma=False,
    )
```

```python
import functools
import math

import jax
import jax.numpy as jnp
from jax import lax
from jax.experimental import pallas as pl
from jax.experimental.pallas import tpu as pltpu
from jax.sharding import PartitionSpec as P

MESH = pl.DeviceIdType.MESH
LANES = 128
LOW = -1e30

OFFSETS = ((0, 0), (1, 0), (-1, 0), (0, 1), (0, -1), (1, 1), (1, -1), (-1, 1), (-1, -1))


def roll_flat(rows, shift_row, shift_col, side_len):
    result = jnp.roll(rows, shift_row * side_len, axis=1)
    if shift_col != 0:
        column = jnp.arange(side_len * side_len, dtype=jnp.int32) % side_len
        edge = 0 if shift_col > 0 else side_len - 1
        wrapped = jnp.roll(result, shift_col - shift_col * side_len, axis=1)
        plain = jnp.roll(result, shift_col, axis=1)
        result = jnp.where((column == edge)[None, :], wrapped, plain)
    return result


def shift_stack(rotated, side_len):
    return jnp.concatenate(
        [roll_flat(rotated, shift_row, shift_col, side_len) for shift_row, shift_col in OFFSETS],
        axis=0,
    )


def unshift_sum(summed_back, rot_count, side_len):
    square = summed_back.reshape(len(OFFSETS), rot_count, side_len * side_len)
    result = jnp.zeros((rot_count, side_len * side_len), jnp.float32)
    for position, offset in enumerate(OFFSETS):
        result = result + roll_flat(square[position], -offset[0], -offset[1], side_len)
    return result


def on_device(images, references, candidates, inv_noise):
    rows_dev, top_count = candidates.shape
    cls_dev, rot_count, pixels = references.shape
    side_len = math.isqrt(pixels)
    shift_count = len(OFFSETS)
    orient_count = rot_count * shift_count
    n_cls = lax.axis_size("cls")
    classes = cls_dev * n_cls
    slot_depth = max(2, (3 * rows_dev * top_count + 2 * classes - 1) // (2 * classes))
    owner_slots = cls_dev * slot_depth
    slots_all = n_cls * owner_slots
    member = jnp.sum(
        (candidates[:, :, None] == jnp.arange(classes, dtype=jnp.int32)[None, None, :]).astype(
            jnp.int32
        ),
        axis=1,
    )
    earlier = jnp.arange(rows_dev)[:, None] > jnp.arange(rows_dev)[None, :]
    before = jnp.sum(earlier.astype(jnp.int32)[:, :, None] * member[None, :, :], axis=1)
    slot_rank = jnp.take_along_axis(before, candidates, axis=1)
    slot_index = candidates // cls_dev * owner_slots + candidates % cls_dev * slot_depth + slot_rank
    flat_slot = slot_index.reshape(-1)
    source = (
        jnp.full((slots_all,), rows_dev, jnp.int32)
        .at[flat_slot]
        .set(jnp.repeat(jnp.arange(rows_dev, dtype=jnp.int32), top_count))
    )
    images_pad = jnp.concatenate([images, jnp.zeros((1, pixels), jnp.bfloat16)], axis=0)
    noise_pad = jnp.concatenate([inv_noise, jnp.zeros((1,), jnp.bfloat16)], axis=0)
    send_img = images_pad[source].reshape(n_cls, owner_slots * pixels)
    send_noise = noise_pad[source].reshape(n_cls, owner_slots)
    recv_img, recv_noise = (
        lax.all_to_all(send_img, "cls", split_axis=0, concat_axis=0, tiled=True),
        lax.all_to_all(send_noise, "cls", split_axis=0, concat_axis=0, tiled=True),
    )
    live_list = []
    class_pos = 0
    rows_img = recv_img.reshape(n_cls * slot_depth, pixels)
    rows_noise = recv_noise.reshape(-1).astype(jnp.float32)
    shifted = shift_stack(references[class_pos], side_len)
    ref_norms = jnp.sum(jnp.square(references[class_pos].astype(jnp.float32)), axis=1)
    products = lax.dot_general(
        rows_img, shifted, (((1,), (1,)), ((), ())), preferred_element_type=jnp.float32
    )
    class_scores = rows_noise[:, None] * (
        products - 0.5 * jnp.tile(ref_norms, shift_count)[None, :]
    )
    rows_list = [rows_img]
    live_list.append(rows_noise > 0)
    score_list = [class_scores]
    send_scores = jnp.concatenate(
        [part_scores.reshape(n_cls, slot_depth * orient_count) for part_scores in score_list],
        axis=1,
    )
    home_scores = lax.all_to_all(send_scores, "cls", split_axis=0, concat_axis=0, tiled=True)
    own_scores = home_scores.reshape(slots_all, orient_count)[slot_index]
    row_peak = jnp.max(own_scores, axis=(1, 2))
    norm_total = jnp.sum(jnp.exp(own_scores - row_peak[:, None, None]), axis=(1, 2))
    home_weights = (
        jnp.exp(own_scores - row_peak[:, None, None]) / norm_total[:, None, None]
    ).astype(jnp.bfloat16)
    slot_weights = (
        jnp.zeros((slots_all, orient_count), jnp.bfloat16)
        .at[flat_slot]
        .set(home_weights.reshape(-1, orient_count))
    )
    weights = lax.all_to_all(
        slot_weights.reshape(n_cls, owner_slots * orient_count),
        "cls",
        split_axis=0,
        concat_axis=0,
        tiled=True,
    )
    weight_rows = [weights.reshape(n_cls * slot_depth, orient_count)]
    class_pos = 0
    row_weights = weight_rows[class_pos]
    summed_back = lax.dot_general(
        row_weights,
        rows_list[class_pos],
        (((0,), (0,)), ((), ())),
        preferred_element_type=jnp.float32,
    )
    sums_list = [unshift_sum(summed_back, rot_count, side_len)]
    weight_list = [
        jnp.sum(row_weights.astype(jnp.float32), axis=0).reshape(shift_count, rot_count).sum(axis=0)
    ]
    local_sums = jnp.stack(sums_list, axis=0)
    local_weights = jnp.stack(weight_list, axis=0)
    class_sums, class_weights = (
        lax.psum_scatter(local_sums, "dp", scatter_dimension=1, tiled=True),
        lax.psum_scatter(local_weights, "dp", scatter_dimension=1, tiled=True),
    )
    return (class_sums, class_weights)


PLANES = 4
SQUARE = 4
BIG = 1e30
PIECES = 4
END = (
    4, 16, 32, 5, 17, 33, 6, 18, 34, 7, 19, 35, 20, 36, 8, 37, 48, 9, 21, 38,
    10, 49, 50, 11, 22, 39, 12, 23, 51, 13, 40, 52, 14, 24, 41, 15, 42, 53, 25, 43,
    26, 54, 27, 44, 28, 55, 29, 45, 46, 56, 30, 47, 57, 58, 31, 59, 60, 61, 62, 63,
)
MID = (
    4, 8, 16, 32, 5, 9, 17, 33, 6, 10, 18, 34, 7, 11, 19, 35, 12, 20, 36, 13,
    24, 40, 14, 37, 48, 15, 21, 41, 25, 38, 42, 49, 22, 50, 26, 39, 23, 43, 27, 51,
    28, 44, 45, 52, 29, 46, 47, 56, 30, 54, 53, 58, 31, 55, 57, 59, 60, 62, 61, 63,
)


def dense_kernel(
    rows_dev, pixels, half, pad, side, n_cls,
    img_ref, cand_ref, noise_ref, ref_ref, sums_ref, tot_ref,
    held, shifted, offset, acc, expo, peaks, wts, back, mine, stats,
    own_sem, send_sem, recv_sem, part_send, part_recv,
    st_send, st_recv,
):
    cls = lax.axis_index("cls")
    d = lax.axis_index("dp")
    z, y, x = cls // 4, (cls // 2) % 2, cls % 2
    other = 1 - d
    me = cls * 2 + d
    n_dev = n_cls * 2
    width = held.shape[2]
    lots = width // LANES
    edges = [q * lots // PIECES * LANES for q in range(PIECES + 1)]
    band = shifted.shape[0] // 3
    tiles = pixels // LANES
    plane_rows = 2 * SQUARE * rows_dev

    def block(bz, by, bx):
        return bz * 4 + by * 2 + bx

    t = z // 2
    order = [z, z + 1 - 2 * (z % 2), 2 - t, 3 - 3 * t]
    x_dev = {"cls": block(z, y, 1 - x), "dp": d}
    y_dev = {"cls": block(z, 1 - y, x), "dp": d}
    in_dev = {"cls": block(1 + z % 2, y, x), "dp": d}
    out_dev = {"cls": block(3 * (z // 2), y, x), "dp": d}
    middle = jnp.logical_or(z == 1, z == 2)
    border = jnp.logical_not(middle)
    core_dev = {"cls": cls, "dp": other}

    barrier = pltpu.get_barrier_semaphore()

    def greet(dev):
        pl.semaphore_signal(barrier, inc=1, device_id=dev, device_id_type=MESH)

    for dev in (x_dev, y_dev, core_dev, in_dev):
        greet(dev)
    pl.when(middle)(lambda: greet(out_dev))

    def slot(b, core=d):
        return (b // SQUARE) * 2 * SQUARE + core * SQUARE + b % SQUARE

    local = pltpu.make_async_copy(img_ref, held.at[slot(cls), :, pl.ds(0, pixels)], own_sem)
    local.start()

    def describe():
        eye = (
            lax.broadcasted_iota(jnp.int32, (rows_dev, rows_dev), 0)
            == lax.broadcasted_iota(jnp.int32, (rows_dev, rows_dev), 1)
        ).astype(jnp.float32).astype(jnp.bfloat16)
        dims = (((1,), (1,)), ((), ()))
        names = lax.dot_general(
            eye, cand_ref[...].astype(jnp.float32).astype(jnp.bfloat16), dims, preferred_element_type=jnp.float32
        )
        noise = jnp.broadcast_to(noise_ref[...].astype(jnp.float32), (8, rows_dev)).astype(jnp.bfloat16)
        level = lax.dot_general(eye, noise, dims, preferred_element_type=jnp.float32)[:, 0:1]
        lanes = lax.broadcasted_iota(jnp.int32, (rows_dev, LANES), 1).astype(jnp.float32)
        named = names[:, 0:1] == lanes
        for k in range(1, cand_ref.shape[0]):
            named = jnp.logical_or(named, names[:, k:k + 1] == lanes)
        held[slot(cls), :, pixels:pixels + LANES] = jnp.where(named, level, 0.0).astype(jnp.bfloat16)

    describe()
    local.wait()

    def moves(first, second):
        row = lax.broadcasted_iota(jnp.int32, (LANES, 2 * LANES), 0)
        col = lax.broadcasted_iota(jnp.int32, (LANES, 2 * LANES), 1)
        step = jnp.where(col < LANES, first, second)
        source = jnp.bitwise_or(jnp.bitwise_and(col, side), jnp.bitwise_and(col + step, side - 1))
        return (row == source).astype(jnp.float32).astype(jnp.bfloat16)

    def left(v):
        return jnp.concatenate([v[:, LANES:], v[:, :LANES]], axis=1)

    def build():
        row = lax.broadcasted_iota(jnp.int32, (pad, 2 * half), 0)
        col = lax.broadcasted_iota(jnp.int32, (pad, 2 * half), 1)
        pick = jnp.logical_and(col == row + d * half, row < half).astype(jnp.float32).astype(jnp.bfloat16)
        width_c = pixels // 8
        for c in range(8):
            cols = pl.ds(c * width_c, width_c)
            back[0:pad, cols] = jnp.dot(pick, ref_ref[0, :, cols], preferred_element_type=jnp.float32)
        for i in range(pad // 8):
            v = back[8 * i:8 * i + 8, :]
            back[pad + 8 * i:pad + 8 * i + 8, :] = pltpu.roll(v, side, 1)
            back[2 * pad + 8 * i:2 * pad + 8 * i + 8, :] = pltpu.roll(v, pixels - side, 1)
        if band > 3 * pad:
            back[3 * pad:band, :] = jnp.zeros((band - 3 * pad, pixels), jnp.float32)
        energy = 0.5 * jnp.sum(jnp.square(back[0:pad, :]), axis=1, keepdims=True)
        spare = lax.broadcasted_iota(jnp.int32, (pad, 1), 0) >= half
        energy = jnp.where(spare, BIG, energy)
        for dy in range(3):
            offset[dy * pad:(dy + 1) * pad, :] = jnp.broadcast_to(energy, (pad, LANES))
        if band > 3 * pad:
            offset[3 * pad:band, :] = jnp.full((band - 3 * pad, LANES), BIG, jnp.float32)
        both = moves(-1, 1)
        for j in range(tiles):
            cols = pl.ds(j * LANES, LANES)
            base = back[0:band, cols].astype(jnp.bfloat16)
            pair = jnp.dot(base, both, preferred_element_type=jnp.float32).astype(jnp.bfloat16)
            shifted[0:band, cols] = base
            shifted[band:2 * band, cols] = pair[:, 0:LANES]
            shifted[2 * band:3 * band, cols] = pair[:, LANES:2 * LANES]

    build()
    pl.semaphore_wait(barrier, 4 + jnp.where(middle, 1, 0))

    def remote(src, dst, send, recv, dev):
        return pltpu.make_async_remote_copy(
            src_ref=src, dst_ref=dst, send_sem=send, recv_sem=recv, device_id=dev, device_id_type=MESH
        )

    def span(b, first, last, core=d):
        return held.at[slot(b, core), :, pl.ds(edges[first], edges[last] - edges[first])]

    sent = {True: [], False: []}

    def one_piece(index, code, dev):
        b, q = where_from(code), code % 4
        ref = span(b, q, q + 1)
        return remote(ref, ref, send_sem.at[index], recv_sem.at[q, b], dev)

    def pass_on(inner, code, dev):
        sent[inner].append(code)
        one_piece(len(sent[inner]) - 1, code, dev).start()

    def where_from(code):
        kind, k = code // 16, code // 4 % 4
        return block(order[k], (y, y, 1 - y, 1 - y)[kind], (x, 1 - x, x, 1 - x)[kind])

    def forward(inner, code):
        kind, k, q = code // 16, code // 4 % 4, code % 4
        low = q < PIECES // 2
        devs = []
        if kind == 0:
            if inner:
                devs = [out_dev, in_dev] if k == 0 else [in_dev if k == 1 else out_dev]
            elif k == 0:
                devs = [in_dev]
            devs = devs + [x_dev, y_dev]
        elif kind == 1 and not low:
            devs = [y_dev]
        elif kind == 2 and low:
            devs = [x_dev]
        for dev in devs:
            pass_on(inner, code, dev)

    def to_core(code):
        b, part = where_from(code), code % 4 // 2
        ref = span(b, 2 * part, 2 * part + 2)
        return remote(ref, ref, part_send.at[code // 4, part], part_recv.at[part, b], core_dev)

    def take(inner, code, done):
        one_piece(0, code, x_dev).wait_recv()
        forward(inner, code)
        if code ^ 1 in done:
            to_core(code).start()

    def wait_core(b):
        for part in range(2):
            ref = span(b, 2 * part, 2 * part + 2, other)
            remote(ref, ref, part_send.at[0, 0], part_recv.at[part, b], core_dev).wait_recv()

    depth = pixels // 4

    def chunk_cols(c):
        return pl.ds(pl.multiple_of(c * depth, depth), depth)

    one = (lax.broadcasted_iota(jnp.int32, (8, LANES), 1) == cls).astype(jnp.float32).astype(jnp.bfloat16)

    def multiply(plane, c):
        first = plane * 2 * SQUARE
        cols = pl.ds(c * depth, depth)
        right = held[pl.ds(first, 2 * SQUARE), :, cols].reshape(plane_rows, depth)
        value = lax.dot_general(
            shifted[:, cols], right, (((1,), (1,)), ((), ())), preferred_element_type=jnp.float32
        )
        acc[...] = value if c == 0 else acc[...] + value

    def score(plane):
        prod = acc[...]
        first = plane * 2 * SQUARE
        meta = held[pl.ds(first, 2 * SQUARE), :, pixels:pixels + LANES].reshape(plane_rows, LANES)
        noise = lax.dot_general(one, meta, (((1,), (1,)), ((), ())), preferred_element_type=jnp.float32)[0:1, :]
        live = noise > 0
        value = noise[None] * (prod.reshape(3, band, plane_rows) - offset[...][None])
        peak = jnp.max(jnp.max(value, axis=0), axis=0, keepdims=True)
        peak = jnp.where(live, peak, LOW)
        grown = jnp.where(live[None], jnp.exp(value - peak[None]), 0.0)
        total = jnp.sum(jnp.sum(grown, axis=0), axis=0, keepdims=True)
        peaks[plane, 0:1, :] = peak
        peaks[plane, 1:2, :] = total
        expo[plane] = grown

    pairs = ((1, 2), (0, 3))

    def stat(m, target, core):
        return remote(mine.at[m], stats.at[m, me], st_send.at[m], st_recv.at[m], {"cls": target, "dp": core})

    def send_stats(m):
        for g, plane in enumerate(pairs[m]):
            mine[m, :, g * plane_rows:(g + 1) * plane_rows] = peaks[plane]
        for step in [*range(4, 8), *range(12, 16), *range(8, 12), *range(4)]:
            far = cls + step
            target = jnp.where(far >= n_cls, far - n_cls, far)
            if step > 0:
                stat(m, target, d).start()
            stat(m, target, other).start()
        stats[m, me] = mine[m]

    def all_of(m, sem):
        ref = stats.at[m, pl.ds(0, n_dev - 1)]
        return pltpu.make_async_copy(ref, ref, sem.at[m])

    def weigh(m):
        all_of(m, st_recv).wait()
        every = stats[m]
        top = jnp.max(every[:, 0:1, :], axis=0)
        norm = jnp.sum(every[:, 1:2, :] * jnp.exp(every[:, 0:1, :] - top[None]), axis=0)
        factor = jnp.exp(mine[m, 0:1, :] - top) / norm
        flat = jnp.zeros((band, plane_rows), jnp.float32)
        for g, plane in enumerate(pairs[m]):
            weight = (expo[plane] * factor[None, :, g * plane_rows:(g + 1) * plane_rows]).astype(jnp.bfloat16)
            for dx in range(3):
                wts[m, dx * band:(dx + 1) * band, g * plane_rows:(g + 1) * plane_rows] = weight[dx]
            flat = flat + jnp.sum(weight.astype(jnp.float32), axis=0)
        return sum(flat[dy * pad:(dy + 1) * pad] for dy in range(3))

    def project(m):
        def part(c, carry):
            cols = pl.ds(c * depth, depth)
            right = jnp.concatenate(
                [
                    held[plane * 2 * SQUARE:(plane + 1) * 2 * SQUARE, :, cols].reshape(plane_rows, depth)
                    for plane in pairs[m]
                ],
                axis=0,
            )
            value = jnp.dot(wts[m], right, preferred_element_type=jnp.float32)
            back[:, cols] = value if m == 0 else back[:, cols] + value
            return carry

        for c in range(4):
            part(c, 0)

    def core_in(k):
        for by in (0, 1):
            for bx in (0, 1):
                wait_core(block(order[k], by, bx))

    def diagonal(k):
        b = block(order[k], 1 - y, 1 - x)
        piece(b, part_a, y_send.at[k], a_recv, x_dev).wait_recv()
        piece(b, part_b, x_send.at[k], b_recv, y_dev).wait_recv()
        go(to_core(3 * PLANES + k, b))

    work = []

    def queue_score(k):
        work.append(lambda: (core_in(k), multiply(order[k], 0), multiply(order[k], 1)))
        work.append(lambda: (multiply(order[k], 2), multiply(order[k], 3), score(order[k])))

    def idle():
        if work:
            work.pop(0)()

    def drain():
        while work:
            idle()

    def send_own(inner):
        for q in range(PIECES):
            forward(inner, q)

    pl.when(border)(lambda: send_own(False))
    pl.when(middle)(lambda: send_own(True))
    to_core(0).start()
    to_core(2).start()
    ready = {}
    for codes in (END, MID):
        for i, code in enumerate(codes):
            ready[code // 4 % 4] = max(ready.get(code // 4 % 4, 0), i)
    for i in range(len(END)):
        pl.when(border)(lambda: take(False, END[i], END[:i]))
        pl.when(middle)(lambda: take(True, MID[i], MID[:i]))
        for k in range(3):
            if i == ready[k] + 2:
                queue_score(k)
                if k == 2:
                    work.append(lambda: send_stats(0))
        if i % 1 == 0:
            idle()
    for k in range(3):
        if len(END) <= ready[k] + 2:
            queue_score(k)
            if k == 2:
                work.append(lambda: send_stats(0))
    drain()
    queue_score(3)
    drain()
    send_stats(1)

    def all_sent(inner):
        for index, code in enumerate(sent[inner]):
            one_piece(index, code, x_dev).wait_send()

    pl.when(border)(lambda: all_sent(False))
    pl.when(middle)(lambda: all_sent(True))
    for code in sorted(set(END + (0, 1, 2, 3))):
        if code % 2 == 0:
            to_core(code).wait_send()
    flat = weigh(0)
    project(0)
    flat = flat + weigh(1)
    project(1)

    both = moves(1, -1)

    def parts(v):
        high = v.astype(jnp.bfloat16)
        return high, (v - high.astype(jnp.float32)).astype(jnp.bfloat16)

    for i in range(pad // 8):
        lines = []
        for dx in range(3):
            same, above, below = (
                back[dx * band + k * pad + 8 * i:dx * band + k * pad + 8 * i + 8, :] for k in range(3)
            )
            lines.append(same + pltpu.roll(left(above) + below, side, 1))
        back[8 * i:8 * i + 8, :] = lines[0]
        back[band + 8 * i:band + 8 * i + 8, :] = lines[1]
        back[2 * band + 8 * i:2 * band + 8 * i + 8, :] = lines[2]
    span_count = 8
    for c in range(0, tiles, span_count):
        total = None
        for dx in (1, 2):
            chunks = [
                back[dx * band:dx * band + pad, (c + u) * LANES:(c + u + 1) * LANES] for u in range(span_count)
            ]
            source = jnp.concatenate(chunks, axis=0)
            move = both[:, (dx - 1) * LANES:dx * LANES]
            value = jnp.dot(
                jnp.concatenate(parts(source), axis=1),
                jnp.concatenate([move, move], axis=0),
                preferred_element_type=jnp.float32,
            )
            total = value if total is None else total + value
        for u in range(span_count):
            value = total[u * pad:(u + 1) * pad] + back[0:pad, (c + u) * LANES:(c + u + 1) * LANES]
            for i in range(pad // 8):
                sums_ref[pl.ds(8 * i * tiles + c + u, 8, stride=tiles), :] = value[8 * i:8 * i + 8]
    column = jnp.sum(flat, axis=1, keepdims=True)
    eye = lax.broadcasted_iota(jnp.int32, (pad, LANES), 0) == lax.broadcasted_iota(jnp.int32, (pad, LANES), 1)
    tot_ref[...] = jnp.sum(jnp.where(eye, column, 0.0), axis=0, keepdims=True)[:, 0:half]
    for m in range(2):
        all_of(m, st_send).wait()


def deliver(rows, sums_ref, tot_ref, sums_out, tot_out, sem):
    copies = [
        pltpu.make_async_copy(sums_ref.at[pl.ds(0, rows)], sums_out, sem.at[0]),
        pltpu.make_async_copy(tot_ref, tot_out, sem.at[1]),
    ]
    for copy in copies:
        copy.start()
    for copy in copies:
        copy.wait()


def dense_on_device(images, references, candidates, inv_noise):
    rows_dev, pixels = images.shape
    n_cls, n_dp = lax.axis_size("cls"), lax.axis_size("dp")
    rot_count = references.shape[1]
    half = rot_count // n_dp
    pad = (half + 7) // 8 * 8
    side = math.isqrt(pixels)
    band = (3 * pad + 15) // 16 * 16
    plane_rows = 2 * SQUARE * rows_dev
    tiles = pixels // LANES
    width = pixels + LANES
    dma = pltpu.SemaphoreType.DMA
    vmem = pl.BlockSpec(memory_space=pltpu.VMEM)
    hbm = pl.BlockSpec(memory_space=pl.ANY)
    sums, totals = pl.pallas_call(
        functools.partial(dense_kernel, rows_dev, pixels, half, pad, side, n_cls),
        out_shape=(
            pltpu.VMEM((pad * tiles, LANES), jnp.float32),
            pltpu.VMEM((1, half), jnp.float32),
        ),
        in_specs=[hbm, vmem, vmem, vmem],
        out_specs=(vmem, vmem),
        scratch_shapes=[
            pltpu.VMEM((n_cls * n_dp, rows_dev, width), jnp.bfloat16),
            pltpu.VMEM((3 * band, pixels), jnp.bfloat16),
            pltpu.VMEM((band, LANES), jnp.float32),
            pltpu.VMEM((3 * band, plane_rows), jnp.float32),
            pltpu.VMEM((PLANES, 3, band, plane_rows), jnp.float32),
            pltpu.VMEM((PLANES, 2, plane_rows), jnp.float32),
            pltpu.VMEM((2, 3 * band, 2 * plane_rows), jnp.bfloat16),
            pltpu.VMEM((3 * band, pixels), jnp.float32),
            pltpu.VMEM((2, 2, 2 * plane_rows), jnp.float32),
            pltpu.VMEM((2, n_cls * n_dp, 2, 2 * plane_rows), jnp.float32),
            dma,
            dma((96,)),
            dma((PIECES, n_cls)),
            dma((4 * PLANES, 2)),
            dma((2, n_cls)),
            dma((2,)),
            dma((2,)),
        ],
        compiler_params=pltpu.CompilerParams(
            collective_id=0, has_side_effects=True, vmem_limit_bytes=56 << 20
        ),
    )(images, candidates.T, inv_noise.reshape(1, rows_dev), references)
    sums, totals = pl.pallas_call(
        functools.partial(deliver, half * tiles),
        out_shape=(
            jax.ShapeDtypeStruct((half * tiles, LANES), jnp.float32),
            jax.ShapeDtypeStruct((1, half), jnp.float32),
        ),
        in_specs=[vmem, vmem],
        out_specs=(hbm, hbm),
        scratch_shapes=[dma((2,))],
    )(*(pltpu.with_memory_space_constraint(v, pltpu.VMEM) for v in (sums, totals)))
    return sums.reshape(1, half, pixels), totals


def solution(mesh):
    placed = (
        P(("cls", "dp"), None),
        P("cls", None, None),
        P(("cls", "dp"), None),
        P(("cls", "dp")),
    )
    n_cls, n_dp = mesh.shape["cls"], mesh.shape["dp"]
    dense = n_cls == PLANES * SQUARE and n_dp == 2
    return jax.shard_map(
        dense_on_device if dense else on_device,
        mesh=mesh,
        in_specs=placed,
        out_specs=(P("cls", "dp", None), P("cls", "dp")),
        check_vma=False,
    )
```
